512 devices in a mesh: dp: 16 (over x_lo, z), fsdp: 32 (over x_hi, y, core).
Axes of the slice: x: 4 (x_hi: 2, x_lo: 2; x = x_hi * 2 + x_lo), y: 8, z: 8, core: 2. Of those that a mesh axis runs over, the one named last changes fastest.
Arguments:
- layer_input: bfloat16 [32768, 8192], P('dp', 'fsdp'), may hold values from -6 to 6
- cotangent: bfloat16 [2, 32768, 1024], P(None, ('dp', 'fsdp')), may hold values from -6 to 6
- candidates: bfloat16 [2, 16, 1024, 512], P(None, 'dp', None, 'fsdp'), may hold values from -0.1875 to 0.1875
- moment_first: float32 [2, 512, 8192], P(None, 'dp', 'fsdp'), may hold values from -0.6 to 0.6
- moment_second: float32 [2, 512, 8192], P(None, 'dp', 'fsdp'), may hold values from 0.0001 to 0.01
- owners: int32 [2], replicated, may hold values from 0 to 15
Outputs:
- update: bfloat16 [2, 1024, 8192], P(None, 'dp', 'fsdp')
- first_next: float32 [2, 512, 8192], P(None, 'dp', 'fsdp')
- second_next: float32 [2, 512, 8192], P(None, 'dp', 'fsdp')
The draws below stay inside these ranges and needn't reach their ends.
Inputs may be any that keep to these rules, and one draw needn't show every extreme that they name: owners[m] names a data-parallel replica.
All inputs are finite; a program needn't handle non-finite values.
Results may differ from the reference program's by a relative error of at most 0.0056.
Values may be sent and summed in bfloat16 or wider, within the bound.
A program may use at most 64 MiB of HBM per device.

```python
import math
import jax
import jax.numpy as jnp
from jax import lax

D = 8192
KV = 1024
RANK = 512
MATS = 2
STEP = 10
TOKENS = 32768
N_DP = 16


def shard_levels(stream_key, shape, pieces, least, high):
    level = 1.0
    for axis_at, blocks in pieces:
        steps = jax.random.uniform(jax.random.fold_in(jax.random.fold_in(stream_key, 6), axis_at), (blocks,), jnp.float32, least / len(pieces), high / len(pieces))
        level = level * jnp.repeat(jnp.exp(steps), shape[axis_at] // blocks).reshape((-1,) + (1,) * (len(shape) - 1 - axis_at))
    return level


def centred(own_key, dims, scale, bound, shards=(), dtype=jnp.bfloat16):
    result = scale * jax.random.normal(own_key, dims, jnp.float32)
    if shards:
        result = result * shard_levels(own_key, dims, shards, -0.22, 0.18)
    return jnp.clip(result, -bound, bound).astype(dtype)


def setup_inputs(seed: int = 0) -> dict:
    splits = jax.random.split(jax.random.key(seed), 7)
    return {
        "layer_input": centred(splits[0], (TOKENS, D), 1.0, 6.0, ((0, 16), (1, 32))),
        "cotangent": centred(splits[1], (MATS, TOKENS, KV), 1.0, 6.0, ((1, 512),)),
        "candidates": centred(splits[2], (MATS, N_DP, KV, RANK), KV ** -0.5, 0.1875, ((1, 16), (3, 32))),
        "moment_first": centred(splits[3], (MATS, RANK, D), 0.1, 0.6, ((1, 16), (2, 32)), jnp.float32),
        "moment_second": jnp.clip(jnp.exp(math.log(0.01) - 4.6051702 * jax.random.uniform(splits[4], (MATS, RANK, D), jnp.float32) ** shard_levels(splits[4], (MATS, RANK, D), ((1, 16), (2, 32)), -0.2, 0.2)), 0.0001, 0.01),
        "owners": jax.random.randint(splits[5], (MATS,), 0, N_DP).astype(jnp.int32),
    }


beta_first = 0.9
beta_second = 0.999
epsilon = 1e-08

def reference(layer_input, cotangent, candidates, moment_first, moment_second, owners):
    inverse_root = 1.0 / jnp.sqrt(jnp.asarray(TOKENS, jnp.float32))
    updates = []
    firsts = []
    seconds = []
    for matrix in range(MATS):
        projector = lax.dynamic_index_in_dim(candidates[matrix], owners[matrix], 0, keepdims=False)
        head_rows = jnp.dot(cotangent[matrix], projector, preferred_element_type=jnp.float32).astype(jnp.bfloat16)
        projected = lax.dot_general(head_rows, layer_input, (((0,), (0,)), ((), ())), preferred_element_type=jnp.float32) * inverse_root
        first = beta_first * moment_first[matrix] + (1.0 - beta_first) * projected
        second = beta_second * moment_second[matrix] + (1.0 - beta_second) * projected * projected
        direction = first / (1.0 - beta_first ** STEP) / (jnp.sqrt(second / (1.0 - beta_second ** STEP)) + epsilon)
        direction = direction.astype(jnp.bfloat16)
        updates.append(jnp.dot(projector, direction, preferred_element_type=jnp.float32).astype(jnp.bfloat16))
        firsts.append(first)
        seconds.append(second)
    return (jnp.stack(updates), jnp.stack(firsts), jnp.stack(seconds))
```

```python
import math

import jax
import jax.numpy as jnp
from jax import lax
from jax.experimental import pallas as pl
from jax.experimental.pallas import tpu as pltpu
from jax.sharding import PartitionSpec as P

MATS = 2
STEP = 10
TOKENS = 32768
NB = 2
NZ = 8
NA = 2
NY = 8
NC = 2
LANES = 128

beta_first = 0.9
beta_second = 0.999
epsilon = 1e-08

MESH = pl.DeviceIdType.MESH


def kernel(
    owners,
    x_hbm,
    c_hbm,
    cand,
    first_hbm,
    second_hbm,
    update_out,
    first_out,
    second_out,
    xbuf,
    cbuf,
    picked,
    pt,
    ht,
    acc,
    rsend,
    rrecv,
    fsend,
    frecv,
    dirs,
    rows,
    rows_t,
    first_in,
    second_in,
    local_sem,
    x_s,
    x_r,
    c_s,
    c_r,
    pick_s,
    pick_r,
    tile_s,
    tile_r,
    slab_s,
    slab_r,
    rows_s,
    rows_r,
    h_s,
    h_r,
    r_s,
    r_r,
    f_s,
    f_r,
    d_s,
    d_r,
):
    d = lax.axis_index("dp")
    f = lax.axis_index("fsdp")
    b, z = d // NZ, d % NZ
    a, y, c = f // (NY * NC), (f // NC) % NY, f % NC
    own_s = a * NC + c

    def rdma(src, dst, send, recv, dp, fsdp):
        return pltpu.make_async_remote_copy(
            src_ref=src, dst_ref=dst, send_sem=send, recv_sem=recv, device_id=(dp, fsdp), device_id_type=MESH
        )

    def arrived(dst, send, recv):
        rdma(dst, dst, send, recv, d, f).wait_recv()

    def sent(src, send, recv):
        rdma(src, src, send, recv, d, f).wait_send()

    barrier = pltpu.get_barrier_semaphore()

    def greet(dp, fsdp):
        pl.semaphore_signal(barrier, inc=1, device_id=(dp, fsdp), device_id_type=MESH)

    @pl.loop(0, NB * NZ)
    def _(k):
        for core in range(NC):

            @pl.when(jnp.logical_or(k != d, core != c))
            def _():
                greet(k, a * (NY * NC) + y * NC + core)

    for k in range(NB):
        for core in range(NC):
            greet(k * NZ + z, (1 - a) * (NY * NC) + y * NC + core)
    for k in range(1, NY):
        greet(d, a * (NY * NC) + ((y + k) % NY) * NC + c)

    loads = [
        pltpu.make_async_copy(x_hbm, xbuf.at[own_s], local_sem.at[0]),
        pltpu.make_async_copy(c_hbm.at[c], cbuf.at[own_s], local_sem.at[1]),
        pltpu.make_async_copy(first_hbm, first_in, local_sem.at[2]),
        pltpu.make_async_copy(second_hbm, second_in, local_sem.at[3]),
    ]
    for load in loads:
        load.start()
    pl.semaphore_wait(barrier, NB * NZ * NC - 1 + NB * NC + NY - 1)

    def pick_copy(m, k):
        return rdma(
            cand.at[m, :, pl.ds(pl.multiple_of(k * LANES, LANES), LANES)],
            picked.at[d],
            pick_s.at[m * NZ + k],
            pick_r.at[d],
            c * NZ + k,
            a * (NY * NC) + y * NC + m,
        )

    def pick_self(m, k):
        return jnp.logical_and(c == m, c * NZ + k == d)

    for m in range(MATS):

        @pl.loop(0, NZ)
        def _(k, m=m):
            @pl.when(jnp.logical_not(pick_self(m, k)))
            def _():
                pick_copy(m, k).start()

            @pl.when(pick_self(m, k))
            def _():
                pltpu.make_async_copy(
                    cand.at[m, :, pl.ds(pl.multiple_of(k * LANES, LANES), LANES)], picked.at[d], pick_r.at[d]
                ).start()

    trio = ((0, 1), (1, 0), (1, 1))

    def trio_at(i):
        da, dc = trio[i]
        return (a + da) % NA, (c + dc) % NC

    def c_copy(i):
        oa, oc = trio_at(i)
        return rdma(c_hbm.at[oc], cbuf.at[own_s], c_s.at[i], c_r.at[own_s], d, oa * (NY * NC) + y * NC + oc)

    def x_copy(i):
        oa, oc = trio_at(i)
        return rdma(x_hbm, xbuf.at[own_s], x_s.at[i], x_r.at[own_s], d, oa * (NY * NC) + y * NC + oc)

    for i in range(3):
        c_copy(i).start()
    for i in range(3):
        x_copy(i).start()

    @pl.loop(0, NB * NZ)
    def _(k):
        arrived(picked.at[k], pick_s.at[0], pick_r.at[k])

    lanes_own = pl.ds(pl.multiple_of(z * LANES, LANES), LANES)
    pt[y, b, :, lanes_own] = picked[owners[c]]

    def tile_copy(k):
        to = (d + k) % (NB * NZ)
        return rdma(
            pt.at[y, b, :, lanes_own], pt.at[y, b, :, lanes_own], tile_s.at[k], tile_r.at[d], to, f
        )

    @pl.loop(1, NB * NZ)
    def _(k):
        tile_copy(k).start()

    @pl.loop(1, NB * NZ)
    def _(k):
        source = (d + k) % (NB * NZ)
        arrived(
            pt.at[y, source // NZ, :, pl.ds(pl.multiple_of((source % NZ) * LANES, LANES), LANES)],
            tile_s.at[0],
            tile_r.at[source],
        )

    def slab_copy(k):
        return rdma(
            pt.at[y], pt.at[y], slab_s.at[k], slab_r.at[y], d, a * (NY * NC) + ((y + k) % NY) * NC + c
        )

    order = (1, 7, 2, 6, 3, 5, 4)
    for k in order:
        slab_copy(k).start()

    loads[1].wait()
    for i in range(3):
        oa, oc = trio_at(i)
        arrived(cbuf.at[oa * NC + oc], c_s.at[0], c_r.at[oa * NC + oc])
    for k in order:
        source = (y + k) % NY
        arrived(pt.at[source], slab_s.at[0], slab_r.at[source])

    tokens = NA * NC * cbuf.shape[1]
    heads = lax.dot_general(
        pt[...].reshape(NY * NB * 16, NZ * LANES),
        cbuf[...].reshape(tokens, NZ * LANES),
        (((1,), (1,)), ((), ())),
        preferred_element_type=jnp.float32,
    )
    ht[y] = heads.astype(jnp.bfloat16).reshape(2, 128, tokens)

    def ring_copy(way, step, q):
        slot = (y - step + 1) % NY if way == 0 else (y + step - 1) % NY
        to = (y + 1) % NY if way == 0 else (y + NY - 1) % NY
        return rdma(
            ht.at[slot, q],
            ht.at[slot, q],
            h_s.at[way, step - 1, q],
            h_r.at[way, step - 1, q],
            d,
            a * (NY * NC) + to * NC + c,
        )

    def ring_slot(way, step):
        return (y - step + NY) % NY if way == 0 else (y + step) % NY

    def ring_arrived(way, step, q):
        arrived(ht.at[ring_slot(way, step), q], h_s.at[0, 0, 0], h_r.at[way, step - 1, q])

    def forward(step):
        for q in range(2):
            for way in range(2):
                if step > 1:
                    ring_arrived(way, step - 1, q)
                if step < 4 or q == way:
                    ring_copy(way, step, q).start()

    def product(slots, start):
        for s in range(NA * NC):
            total = None if start else acc[s]
            for slot in slots:
                part = jnp.dot(
                    ht[slot].reshape(256, tokens),
                    xbuf[s, :, slot].reshape(tokens, 256),
                    preferred_element_type=jnp.float32,
                )
                total = part if total is None else total + part
            acc[s] = total

    def rows_copy(i):
        oa, oc = trio_at(i)
        return rdma(
            pt.at[:, :, :, pl.ds(pl.multiple_of((d // 2) * LANES, LANES), LANES)],
            rows.at[c, a],
            rows_s.at[i],
            rows_r.at[own_s],
            d,
            oa * (NY * NC) + y * NC + oc,
        )

    forward(1)
    for i in range(3):
        rows_copy(i).start()
    rows[c, a] = pt[:, :, :, pl.ds(pl.multiple_of((d // 2) * LANES, LANES), LANES)]
    forward(2)
    loads[0].wait()
    for i in range(3):
        oa, oc = trio_at(i)
        arrived(xbuf.at[oa * NC + oc], x_s.at[0], x_r.at[oa * NC + oc])
    product((y, ring_slot(0, 1), ring_slot(1, 1)), True)
    forward(3)
    product((ring_slot(0, 2), ring_slot(1, 2)), False)
    forward(4)
    product((ring_slot(0, 3), ring_slot(1, 3)), False)
    ring_arrived(0, 4, 0)
    ring_arrived(1, 4, 1)
    product((ring_slot(0, 4),), False)

    for k in range(NZ):
        for s in range(NA * NC):
            rsend[k, s] = acc[s, 32 * k : 32 * k + 32, :].astype(jnp.bfloat16)

    def r_copy(k):
        to = (z + k) % NZ
        return rdma(rsend.at[to], rrecv.at[z], r_s.at[k], r_r.at[z], b * NZ + to, f)

    for k in (4, 3, 5, 2, 6, 1, 7):
        r_copy(k).start()
    for i in range(3):
        oa, oc = trio_at(i)
        arrived(rows.at[oc, oa], rows_s.at[0], rows_r.at[oa * NC + oc])
    for m in range(MATS):
        rows_t[m] = rows[m].reshape(512, LANES).T
    loads[2].wait()
    loads[3].wait()
    total = rsend[z].astype(jnp.float32)
    for k in order:
        source = (z + k) % NZ
        arrived(rrecv.at[source], r_s.at[0], r_r.at[source])
        total = total + rrecv[source].astype(jnp.float32)
    fsend[...] = total.astype(jnp.bfloat16)

    def f_self(s):
        return jnp.logical_and(s == own_s, a == b)

    def f_copy(s):
        return rdma(
            fsend.at[s],
            frecv.at[b, c],
            f_s.at[s],
            f_r.at[b * NC + c],
            a * NZ + z,
            (s // NC) * (NY * NC) + y * NC + s % NC,
        )

    for s in range(NA * NC):

        @pl.when(jnp.logical_not(f_self(s)))
        def _(s=s):
            f_copy(s).start()

        @pl.when(f_self(s))
        def _(s=s):
            pltpu.make_async_copy(fsend.at[s], frecv.at[b, c], f_r.at[b * NC + c]).start()

    for k in range(NB):
        for m in range(NC):
            arrived(frecv.at[k, m], f_s.at[0], f_r.at[k * NC + m])

    inverse_root = 1.0 / math.sqrt(TOKENS)
    projected = (frecv[0].astype(jnp.float32) + frecv[1].astype(jnp.float32)) * inverse_root
    first = beta_first * first_in[...] + (1.0 - beta_first) * projected
    second = beta_second * second_in[...] + (1.0 - beta_second) * projected * projected
    direction = (
        first / (1.0 - beta_first**STEP) / (jnp.sqrt(second / (1.0 - beta_second**STEP)) + epsilon)
    )
    dirs[d] = direction.astype(jnp.bfloat16)

    def d_copy(k):
        return rdma(dirs.at[d], dirs.at[d], d_s.at[k], d_r.at[d], (d + k) % (NB * NZ), f)

    @pl.loop(1, NB * NZ)
    def _(k):
        d_copy(k).start()

    first_out[...] = first
    second_out[...] = second

    @pl.loop(1, NB * NZ)
    def _(k):
        source = (d + k) % (NB * NZ)
        arrived(dirs.at[source], d_s.at[0], d_r.at[source])

    for m in range(MATS):
        update_out[m] = jnp.dot(
            rows_t[m, pl.ds(pl.multiple_of((d % 2) * 64, 64), 64), :],
            dirs[:, m].reshape(512, 256),
            preferred_element_type=jnp.float32,
        ).astype(jnp.bfloat16)

    for m in range(MATS):

        @pl.loop(0, NZ)
        def _(k, m=m):
            @pl.when(jnp.logical_not(pick_self(m, k)))
            def _():
                pick_copy(m, k).wait_send()

    for i in range(3):
        c_copy(i).wait_send()
        x_copy(i).wait_send()
        rows_copy(i).wait_send()

    @pl.loop(1, NB * NZ)
    def _(k):
        tile_copy(k).wait_send()
        d_copy(k).wait_send()

    for k in order:
        slab_copy(k).wait_send()
        r_copy(k).wait_send()
    for step in range(1, 5):
        for q in range(2):
            for way in range(2):
                if step < 4 or q == way:
                    ring_copy(way, step, q).wait_send()
    for s in range(NA * NC):

        @pl.when(jnp.logical_not(f_self(s)))
        def _(s=s):
            f_copy(s).wait_send()


def on_device(layer_input, cotangent, candidates, moment_first, moment_second, owners):
    bf16, f32 = jnp.bfloat16, jnp.float32
    x = layer_input.reshape(NA, NY, 128, 256)
    cand = jnp.swapaxes(candidates[:, 0], 1, 2)
    vmem = pl.BlockSpec(memory_space=pltpu.VMEM)
    hbm = pl.BlockSpec(memory_space=pl.ANY)
    sem = pltpu.SemaphoreType.DMA
    return pl.pallas_call(
        kernel,
        out_shape=(
            jax.ShapeDtypeStruct((MATS, 64, 256), bf16),
            jax.ShapeDtypeStruct((MATS, 32, 256), f32),
            jax.ShapeDtypeStruct((MATS, 32, 256), f32),
        ),
        in_specs=[pl.BlockSpec(memory_space=pltpu.SMEM), hbm, hbm, hbm, hbm, hbm],
        out_specs=(vmem, vmem, vmem),
        scratch_shapes=[
            pltpu.VMEM((4, NA, NY, 128, 256), bf16),
            pltpu.VMEM((4, 64, 1024), bf16),
            pltpu.VMEM((16, 16, LANES), bf16),
            pltpu.VMEM((NY, NB, 16, 1024), bf16),
            pltpu.VMEM((NY, 2, 128, 256), bf16),
            pltpu.VMEM((4, 256, 256), f32),
            pltpu.VMEM((NZ, 4, 32, 256), bf16),
            pltpu.VMEM((NZ, 4, 32, 256), bf16),
            pltpu.VMEM((4, 32, 256), bf16),
            pltpu.VMEM((NB, MATS, 32, 256), bf16),
            pltpu.VMEM((16, MATS, 32, 256), bf16),
            pltpu.VMEM((MATS, NA, NY, NB, 16, LANES), bf16),
            pltpu.VMEM((MATS, LANES, 512), bf16),
            pltpu.VMEM((MATS, 32, 256), f32),
            pltpu.VMEM((MATS, 32, 256), f32),
            sem((4,)),
            sem((3,)),
            sem((4,)),
            sem((3,)),
            sem((4,)),
            sem((16,)),
            sem((16,)),
            sem((16,)),
            sem((16,)),
            sem((NY,)),
            sem((NY,)),
            sem((3,)),
            sem((4,)),
            sem((2, 4, 2)),
            sem((2, 4, 2)),
            sem((NZ,)),
            sem((NZ,)),
            sem((4,)),
            sem((4,)),
            sem((16,)),
            sem((16,)),
        ],
        compiler_params=pltpu.CompilerParams(
            collective_id=0, has_side_effects=True, vmem_limit_bytes=67043328
        ),
    )(owners, x, cotangent, cand, moment_first, moment_second)


def solution(mesh):
    placed = (
        P("dp", "fsdp"),
        P(None, ("dp", "fsdp"), None),
        P(None, "dp", None, "fsdp"),
        P(None, "dp", "fsdp"),
        P(None, "dp", "fsdp"),
        P(),
    )
    return jax.shard_map(
        on_device,
        mesh=mesh,
        in_specs=placed,
        out_specs=(P(None, "dp", "fsdp"), P(None, "dp", "fsdp"), P(None, "dp", "fsdp")),
        check_vma=False,
    )
```

```python
import math

import jax
import jax.numpy as jnp
from jax import lax
from jax.experimental import pallas as pl
from jax.experimental.pallas import tpu as pltpu
from jax.sharding import PartitionSpec as P

MATS = 2
STEP = 10
TOKENS = 32768
NB = 2
NZ = 8
NA = 2
NY = 8
NC = 2
LANES = 128

beta_first = 0.9
beta_second = 0.999
epsilon = 1e-08

MESH = pl.DeviceIdType.MESH


def kernel(
    owners,
    x_hbm,
    c_hbm,
    cand,
    first_hbm,
    second_hbm,
    update_out,
    first_out,
    second_out,
    xbuf,
    cbuf,
    picked,
    pt,
    ht,
    acc,
    rsend,
    rrecv,
    fsend,
    frecv,
    dirs,
    rows,
    rows_t,
    first_in,
    second_in,
    local_sem,
    x_s,
    x_r,
    c_s,
    c_r,
    pick_s,
    pick_r,
    tile_s,
    tile_r,
    slab_s,
    slab_r,
    rows_s,
    rows_r,
    h_s,
    h_r,
    r_s,
    r_r,
    f_s,
    f_r,
    d_s,
    d_r,
):
    d = lax.axis_index("dp")
    f = lax.axis_index("fsdp")
    b, z = d // NZ, d % NZ
    a, y, c = f // (NY * NC), (f // NC) % NY, f % NC
    own_s = a * NC + c

    def rdma(src, dst, send, recv, dp, fsdp):
        return pltpu.make_async_remote_copy(
            src_ref=src, dst_ref=dst, send_sem=send, recv_sem=recv, device_id=(dp, fsdp), device_id_type=MESH
        )

    def arrived(dst, send, recv):
        rdma(dst, dst, send, recv, d, f).wait_recv()

    def sent(src, send, recv):
        rdma(src, src, send, recv, d, f).wait_send()

    barrier = pltpu.get_barrier_semaphore()
    leaving = []

    def greet(dp, fsdp):
        pl.semaphore_signal(barrier, inc=1, device_id=(dp, fsdp), device_id_type=MESH)

    @pl.loop(0, NB * NZ)
    def _(k):
        for core in range(NC):

            @pl.when(jnp.logical_or(k != d, core != c))
            def _():
                greet(k, a * (NY * NC) + y * NC + core)

    for k in range(NB):
        for core in range(NC):
            greet(k * NZ + z, (1 - a) * (NY * NC) + y * NC + core)
    for k in range(1, NY):
        greet(d, a * (NY * NC) + ((y + k) % NY) * NC + c)

    loads = [
        pltpu.make_async_copy(x_hbm, xbuf.at[own_s], local_sem.at[0]),
        pltpu.make_async_copy(c_hbm.at[c], cbuf.at[own_s], local_sem.at[1]),
        pltpu.make_async_copy(first_hbm, first_in, local_sem.at[2]),
        pltpu.make_async_copy(second_hbm, second_in, local_sem.at[3]),
    ]
    for load in loads:
        load.start()
    pl.semaphore_wait(barrier, NB * NZ * NC - 1 + NB * NC + NY - 1)

    def pick_copy(m, k):
        return rdma(
            cand.at[m, :, pl.ds(pl.multiple_of((k % NZ) * LANES, LANES), LANES)],
            picked.at[d, c],
            pick_s.at[m, k],
            pick_r.at[d, c],
            k,
            a * (NY * NC) + y * NC + m,
        )

    def pick_self(m, k):
        return jnp.logical_and(c == m, k == d)

    for m in range(MATS):

        @pl.loop(0, NB * NZ)
        def _(k, m=m):
            @pl.when(jnp.logical_not(pick_self(m, k)))
            def _():
                pick_copy(m, k).start()

    lanes_own = pl.ds(pl.multiple_of(z * LANES, LANES), LANES)
    pick_own = pltpu.make_async_copy(cand.at[c, :, lanes_own], picked.at[d, c], pick_r.at[d, c])
    pick_own.start()

    def picks_left():
        for m in range(MATS):

            @pl.loop(0, NB * NZ)
            def _(k, m=m):
                @pl.when(jnp.logical_not(pick_self(m, k)))
                def _():
                    pick_copy(m, k).wait_send()

    leaving.append(picks_left)

    trio = ((0, 1), (1, 0), (1, 1))

    def trio_at(i):
        da, dc = trio[i]
        return (a + da) % NA, (c + dc) % NC

    def c_copy(i):
        oa, oc = trio_at(i)
        return rdma(c_hbm.at[oc], cbuf.at[own_s], c_s.at[i], c_r.at[own_s], d, oa * (NY * NC) + y * NC + oc)

    def x_copy(half, away):
        oa, oc = (1 - a, c) if away else (a, 1 - c)
        return rdma(
            x_hbm.at[half],
            xbuf.at[own_s, half],
            x_s.at[half, away],
            x_r.at[own_s, half],
            d,
            oa * (NY * NC) + y * NC + oc,
        )

    far_s = (1 - a) * NC + c

    def x_pass(half):
        return rdma(
            xbuf.at[far_s, half],
            xbuf.at[far_s, half],
            x_s.at[half, 2],
            x_r.at[far_s, half],
            d,
            a * (NY * NC) + y * NC + 1 - c,
        )

    for i in range(3):
        c_copy(i).start()
        leaving.append(c_copy(i).wait_send)
    for half in range(NA):
        x_copy(half, 1).start()
        leaving.append(x_copy(half, 1).wait_send)
    for half in range(NA):
        x_copy(half, 0).start()
        leaving.append(x_copy(half, 0).wait_send)

    for core in range(NC):

        @pl.loop(0, NB * NZ)
        def _(k, core=core):
            arrived(picked.at[k, core], pick_s.at[0, 0], pick_r.at[k, core])

    pt[y, :, :, lanes_own] = picked[owners[c]]

    def tile_copy(k):
        return rdma(
            pt.at[y, :, :, lanes_own],
            pt.at[y, :, :, lanes_own],
            tile_s.at[k],
            tile_r.at[z],
            b * NZ + (z + k) % NZ,
            f,
        )

    order = (1, 7, 2, 6, 3, 5, 4)
    for k in order:
        tile_copy(k).start()
        leaving.append(tile_copy(k).wait_send)
    for k in order:
        source = (z + k) % NZ
        arrived(
            pt.at[y, :, :, pl.ds(pl.multiple_of(source * LANES, LANES), LANES)], tile_s.at[0], tile_r.at[source]
        )

    def slab_copy(k):
        return rdma(
            pt.at[y], pt.at[y], slab_s.at[k], slab_r.at[y], d, a * (NY * NC) + ((y + k) % NY) * NC + c
        )

    for k in order:
        slab_copy(k).start()
        leaving.append(slab_copy(k).wait_send)

    loads[1].wait()
    for i in range(3):
        oa, oc = trio_at(i)
        arrived(cbuf.at[oa * NC + oc], c_s.at[0], c_r.at[oa * NC + oc])
    for k in order:
        source = (y + k) % NY
        arrived(pt.at[source], slab_s.at[0], slab_r.at[source])

    tokens = NA * NC * cbuf.shape[1]
    heads = lax.dot_general(
        pt[...].reshape(NY * NB * 16, NZ * LANES),
        cbuf[...].reshape(tokens, NZ * LANES),
        (((1,), (1,)), ((), ())),
        preferred_element_type=jnp.float32,
    )
    ht[y] = heads.astype(jnp.bfloat16).reshape(2, 128, tokens)

    def ring_copy(way, step, q):
        slot = (y - step + 1) % NY if way == 0 else (y + step - 1) % NY
        to = (y + 1) % NY if way == 0 else (y + NY - 1) % NY
        return rdma(
            ht.at[slot, q],
            ht.at[slot, q],
            h_s.at[way, step - 1, q],
            h_r.at[way, step - 1, q],
            d,
            a * (NY * NC) + to * NC + c,
        )

    def ring_slot(way, step):
        return (y - step + NY) % NY if way == 0 else (y + step) % NY

    def ring_arrived(way, step, q):
        arrived(ht.at[ring_slot(way, step), q], h_s.at[0, 0, 0], h_r.at[way, step - 1, q])

    def forward(step):
        for q in range(2):
            for way in range(2):
                if step > 1:
                    ring_arrived(way, step - 1, q)
                if step < 4 or q == way:
                    ring_copy(way, step, q).start()
                    leaving.append(ring_copy(way, step, q).wait_send)

    def product(slots, start):
        for s in range(NA * NC):
            total = None if start else acc[s]
            for slot in slots:
                part = jnp.dot(
                    ht[slot].reshape(256, tokens),
                    xbuf[s, :, slot].reshape(tokens, 256),
                    preferred_element_type=jnp.float32,
                )
                total = part if total is None else total + part
            acc[s] = total

    def rows_copy(i):
        oa, oc = trio_at(i)
        return rdma(
            pt.at[:, :, :, pl.ds(pl.multiple_of((d // 2) * LANES, LANES), LANES)],
            rows.at[c, a],
            rows_s.at[i],
            rows_r.at[own_s],
            d,
            oa * (NY * NC) + y * NC + oc,
        )

    forward(1)
    for i in range(3):
        rows_copy(i).start()
        leaving.append(rows_copy(i).wait_send)
    rows[c, a] = pt[:, :, :, pl.ds(pl.multiple_of((d // 2) * LANES, LANES), LANES)]
    for half in range(NA):
        arrived(xbuf.at[far_s, half], x_s.at[0, 0], x_r.at[far_s, half])
        x_pass(half).start()
        leaving.append(x_pass(half).wait_send)
    forward(2)
    forward(3)
    loads[0].wait()
    for half in range(NA):
        for from_s in (a * NC + 1 - c, (1 - a) * NC + 1 - c):
            arrived(xbuf.at[from_s, half], x_s.at[0, 0], x_r.at[from_s, half])
    product((y, ring_slot(0, 1), ring_slot(1, 1)), True)
    forward(4)
    product((ring_slot(0, 2), ring_slot(1, 2), ring_slot(0, 3), ring_slot(1, 3)), False)
    ring_arrived(0, 4, 0)
    ring_arrived(1, 4, 1)
    product((ring_slot(0, 4),), False)

    for k in range(NZ):
        for s in range(NA * NC):
            rsend[k, s] = acc[s, 32 * k : 32 * k + 32, :].astype(jnp.bfloat16)

    def r_copy(k):
        to = (z + k) % NZ
        return rdma(rsend.at[to], rrecv.at[z], r_s.at[k], r_r.at[z], b * NZ + to, f)

    for k in (4, 3, 5, 2, 6, 1, 7):
        r_copy(k).start()
        leaving.append(r_copy(k).wait_send)
    for i in range(3):
        oa, oc = trio_at(i)
        arrived(rows.at[oc, oa], rows_s.at[0], rows_r.at[oa * NC + oc])
    for m in range(MATS):
        rows_t[m] = rows[m].reshape(512, LANES).T
    loads[2].wait()
    loads[3].wait()
    total = rsend[z].astype(jnp.float32)
    for k in order:
        source = (z + k) % NZ
        arrived(rrecv.at[source], r_s.at[0], r_r.at[source])
        total = total + rrecv[source].astype(jnp.float32)
    fsend[...] = total.astype(jnp.bfloat16)

    def f_self(s):
        return jnp.logical_and(s == own_s, a == b)

    def f_copy(s):
        return rdma(
            fsend.at[s],
            frecv.at[b, c],
            f_s.at[s],
            f_r.at[b * NC + c],
            a * NZ + z,
            (s // NC) * (NY * NC) + y * NC + s % NC,
        )

    for s in range(NA * NC):

        @pl.when(jnp.logical_not(f_self(s)))
        def _(s=s):
            f_copy(s).start()

        @pl.when(f_self(s))
        def _(s=s):
            pltpu.make_async_copy(fsend.at[s], frecv.at[b, c], f_r.at[b * NC + c]).start()

    def f_left():
        for s in range(NA * NC):

            @pl.when(jnp.logical_not(f_self(s)))
            def _(s=s):
                f_copy(s).wait_send()

    leaving.append(f_left)

    for k in range(NB):
        for m in range(NC):
            arrived(frecv.at[k, m], f_s.at[0], f_r.at[k * NC + m])

    inverse_root = 1.0 / math.sqrt(TOKENS)
    projected = (frecv[0].astype(jnp.float32) + frecv[1].astype(jnp.float32)) * inverse_root
    first = beta_first * first_in[...] + (1.0 - beta_first) * projected
    second = beta_second * second_in[...] + (1.0 - beta_second) * projected * projected
    direction = (
        first / (1.0 - beta_first**STEP) / (jnp.sqrt(second / (1.0 - beta_second**STEP)) + epsilon)
    )
    dirs[d] = direction.astype(jnp.bfloat16)

    def d_copy(k):
        return rdma(dirs.at[d], dirs.at[d], d_s.at[k], d_r.at[d], (d + k) % (NB * NZ), f)

    @pl.loop(1, NB * NZ)
    def _(k):
        d_copy(k).start()

    def dirs_left():
        @pl.loop(1, NB * NZ)
        def _(k):
            d_copy(k).wait_send()

    leaving.append(dirs_left)

    first_out[...] = first
    second_out[...] = second

    @pl.loop(1, NB * NZ)
    def _(k):
        source = (d + k) % (NB * NZ)
        arrived(dirs.at[source], d_s.at[0], d_r.at[source])

    for m in range(MATS):
        update_out[m] = jnp.dot(
            rows_t[m, pl.ds(pl.multiple_of((d % 2) * 64, 64), 64), :],
            dirs[:, m].reshape(512, 256),
            preferred_element_type=jnp.float32,
        ).astype(jnp.bfloat16)

    for wait in leaving:
        wait()


def on_device(layer_input, cotangent, candidates, moment_first, moment_second, owners):
    bf16, f32 = jnp.bfloat16, jnp.float32
    x = layer_input.reshape(NA, NY, 128, 256)
    cand = jnp.swapaxes(candidates[:, 0], 1, 2)
    vmem = pl.BlockSpec(memory_space=pltpu.VMEM)
    hbm = pl.BlockSpec(memory_space=pl.ANY)
    sem = pltpu.SemaphoreType.DMA
    return pl.pallas_call(
        kernel,
        out_shape=(
            jax.ShapeDtypeStruct((MATS, 64, 256), bf16),
            jax.ShapeDtypeStruct((MATS, 32, 256), f32),
            jax.ShapeDtypeStruct((MATS, 32, 256), f32),
        ),
        in_specs=[pl.BlockSpec(memory_space=pltpu.SMEM), hbm, hbm, hbm, hbm, hbm],
        out_specs=(vmem, vmem, vmem),
        scratch_shapes=[
            pltpu.VMEM((4, NA, NY, 128, 256), bf16),
            pltpu.VMEM((4, 64, 1024), bf16),
            pltpu.VMEM((16, NC, 16, LANES), bf16),
            pltpu.VMEM((NY, NB, 16, 1024), bf16),
            pltpu.VMEM((NY, 2, 128, 256), bf16),
            pltpu.VMEM((4, 256, 256), f32),
            pltpu.VMEM((NZ, 4, 32, 256), bf16),
            pltpu.VMEM((NZ, 4, 32, 256), bf16),
            pltpu.VMEM((4, 32, 256), bf16),
            pltpu.VMEM((NB, MATS, 32, 256), bf16),
            pltpu.VMEM((16, MATS, 32, 256), bf16),
            pltpu.VMEM((MATS, NA, NY, NB, 16, LANES), bf16),
            pltpu.VMEM((MATS, LANES, 512), bf16),
            pltpu.VMEM((MATS, 32, 256), f32),
            pltpu.VMEM((MATS, 32, 256), f32),
            sem((4,)),
            sem((NA, 3)),
            sem((4, NA)),
            sem((3,)),
            sem((4,)),
            sem((MATS, 16)),
            sem((16, NC)),
            sem((NZ,)),
            sem((NZ,)),
            sem((NY,)),
            sem((NY,)),
            sem((3,)),
            sem((4,)),
            sem((2, 4, 2)),
            sem((2, 4, 2)),
            sem((NZ,)),
            sem((NZ,)),
            sem((4,)),
            sem((4,)),
            sem((16,)),
            sem((16,)),
        ],
        compiler_params=pltpu.CompilerParams(
            collective_id=0, has_side_effects=True, vmem_limit_bytes=67043328
        ),
    )(owners, x, cotangent, cand, moment_first, moment_second)


def solution(mesh):
    placed = (
        P("dp", "fsdp"),
        P(None, ("dp", "fsdp"), None),
        P(None, "dp", None, "fsdp"),
        P(None, "dp", "fsdp"),
        P(None, "dp", "fsdp"),
        P(),
    )
    return jax.shard_map(
        on_device,
        mesh=mesh,
        in_specs=placed,
        out_specs=(P(None, "dp", "fsdp"), P(None, "dp", "fsdp"), P(None, "dp", "fsdp")),
        check_vma=False,
    )
```

```python
import math

import jax
import jax.numpy as jnp
from jax import lax
from jax.experimental import pallas as pl
from jax.experimental.pallas import tpu as pltpu
from jax.sharding import PartitionSpec as P

MATS = 2
STEP = 10
TOKENS = 32768
NB = 2
NZ = 8
NA = 2
NY = 8
NC = 2
LANES = 128

beta_first = 0.9
beta_second = 0.999
epsilon = 1e-08

MESH = pl.DeviceIdType.MESH


def kernel(
    owners,
    x_hbm,
    c_hbm,
    cand,
    first_hbm,
    second_hbm,
    update_out,
    first_out,
    second_out,
    xbuf,
    cbuf,
    picked,
    pt,
    ht,
    acc,
    rsend,
    rrecv,
    fsend,
    frecv,
    dirs,
    rows,
    rows_t,
    first_in,
    second_in,
    local_sem,
    x_s,
    x_r,
    c_s,
    c_r,
    pick_s,
    pick_r,
    tile_s,
    tile_r,
    slab_s,
    slab_r,
    rows_s,
    rows_r,
    h_s,
    h_r,
    r_s,
    r_r,
    f_s,
    f_r,
    d_s,
    d_r,
    p_s,
):
    d = lax.axis_index("dp")
    f = lax.axis_index("fsdp")
    b, z = d // NZ, d % NZ
    a, y, c = f // (NY * NC), (f // NC) % NY, f % NC
    own_s = a * NC + c

    def rdma(src, dst, send, recv, dp, fsdp):
        return pltpu.make_async_remote_copy(
            src_ref=src, dst_ref=dst, send_sem=send, recv_sem=recv, device_id=(dp, fsdp), device_id_type=MESH
        )

    def arrived(dst, send, recv):
        rdma(dst, dst, send, recv, d, f).wait_recv()

    def sent(src, send, recv):
        rdma(src, src, send, recv, d, f).wait_send()

    barrier = pltpu.get_barrier_semaphore()
    leaving = []

    def greet(dp, fsdp):
        pl.semaphore_signal(barrier, inc=1, device_id=(dp, fsdp), device_id_type=MESH)

    @pl.loop(0, NB * NZ)
    def _(k):
        for core in range(NC):

            @pl.when(jnp.logical_or(k != d, core != c))
            def _():
                greet(k, a * (NY * NC) + y * NC + core)

    for k in range(NB):
        for core in range(NC):
            greet(k * NZ + z, (1 - a) * (NY * NC) + y * NC + core)
    for k in range(1, NY):
        greet(d, a * (NY * NC) + ((y + k) % NY) * NC + c)

    loads = [
        pltpu.make_async_copy(x_hbm, xbuf.at[own_s], local_sem.at[0]),
        pltpu.make_async_copy(c_hbm.at[c], cbuf.at[own_s], local_sem.at[1]),
        pltpu.make_async_copy(first_hbm, first_in, local_sem.at[2]),
        pltpu.make_async_copy(second_hbm, second_in, local_sem.at[3]),
    ]
    for load in loads:
        load.start()
    pl.semaphore_wait(barrier, NB * NZ * NC - 1 + NB * NC + NY - 1)

    def pick_copy(m, k):
        return rdma(
            cand.at[m, :, pl.ds(pl.multiple_of((k % NZ) * LANES, LANES), LANES)],
            picked.at[d, c],
            pick_s.at[m, k],
            pick_r.at[d, c],
            k,
            a * (NY * NC) + y * NC + m,
        )

    def pick_self(m, k):
        return jnp.logical_and(c == m, k == d)

    for m in range(MATS):

        @pl.loop(0, NB * NZ)
        def _(k, m=m):
            @pl.when(jnp.logical_not(pick_self(m, k)))
            def _():
                pick_copy(m, k).start()

    lanes_own = pl.ds(pl.multiple_of(z * LANES, LANES), LANES)
    pick_own = pltpu.make_async_copy(cand.at[c, :, lanes_own], picked.at[d, c], pick_r.at[d, c])
    pick_own.start()

    def picks_left():
        for m in range(MATS):

            @pl.loop(0, NB * NZ)
            def _(k, m=m):
                @pl.when(jnp.logical_not(pick_self(m, k)))
                def _():
                    pick_copy(m, k).wait_send()

    leaving.append(picks_left)

    trio = ((0, 1), (1, 0), (1, 1))

    def trio_at(i):
        da, dc = trio[i]
        return (a + da) % NA, (c + dc) % NC

    def c_copy(i):
        oa, oc = trio_at(i)
        return rdma(c_hbm.at[oc], cbuf.at[own_s], c_s.at[i], c_r.at[own_s], d, oa * (NY * NC) + y * NC + oc)

    def x_copy(half, away):
        oa, oc = (1 - a, c) if away else (a, 1 - c)
        return rdma(
            x_hbm.at[half],
            xbuf.at[own_s, half],
            x_s.at[half, away],
            x_r.at[own_s, half],
            d,
            oa * (NY * NC) + y * NC + oc,
        )

    far_s = (1 - a) * NC + c

    def x_pass(half):
        return rdma(
            xbuf.at[far_s, half],
            xbuf.at[far_s, half],
            x_s.at[half, 2],
            x_r.at[far_s, half],
            d,
            a * (NY * NC) + y * NC + 1 - c,
        )

    for i in range(3):
        c_copy(i).start()
        leaving.append(c_copy(i).wait_send)
    for half in range(NA):
        x_copy(half, 1).start()
        leaving.append(x_copy(half, 1).wait_send)
    for half in range(NA):
        x_copy(half, 0).start()
        leaving.append(x_copy(half, 0).wait_send)

    for core in range(NC):

        @pl.loop(0, NB * NZ)
        def _(k, core=core):
            arrived(picked.at[k, core], pick_s.at[0, 0], pick_r.at[k, core])

    pt[y, :, :, lanes_own] = picked[owners[c]]
    order = (1, 7, 2, 6, 3, 5, 4)
    waves = range(2)

    def along_y(k):
        return d, a * (NY * NC) + ((y + k) % NY) * NC + c

    def along_z(k):
        return b * NZ + (z + k) % NZ, f

    def tile_copy(h, k):
        tile = pt.at[y, h, :, lanes_own]
        to = along_y(k) if h else along_z(k)
        return rdma(tile, tile, tile_s.at[h, k], tile_r.at[h, y if h else z], *to)

    def tile_arrived(h, k):
        source = ((y if h else z) + k) % NZ
        lanes = lanes_own if h else pl.ds(pl.multiple_of(source * LANES, LANES), LANES)
        arrived(pt.at[source if h else y, h, :, lanes], tile_s.at[0, 0], tile_r.at[h, source])

    def slab_copy(h, k):
        slab = pt.at[:, h, :, lanes_own] if h else pt.at[y, h]
        to = along_z(k) if h else along_y(k)
        return rdma(slab, slab, slab_s.at[h, k], slab_r.at[h, z if h else y], *to)

    def slab_arrived(h, k):
        source = ((z if h else y) + k) % NZ
        lanes = pl.ds(pl.multiple_of(source * LANES, LANES), LANES)
        arrived(pt.at[:, h, :, lanes] if h else pt.at[source, h], slab_s.at[0, 0], slab_r.at[h, source])

    for h in waves:
        for k in order:
            tile_copy(h, k).start()
            leaving.append(tile_copy(h, k).wait_send)
    for h in waves:
        for k in order:
            tile_arrived(h, k)
        for k in order:
            slab_copy(h, k).start()
            leaving.append(slab_copy(h, k).wait_send)

    tokens = NA * NC * cbuf.shape[1]

    def ring_slot(way, step):
        return (y - step + NY) % NY if way == 0 else (y + step) % NY

    def ring_copy(h, way, step):
        piece = ht.at[ring_slot(way, step - 1), h]
        to = along_y(1 if way == 0 else NY - 1)
        return rdma(piece, piece, h_s.at[h, way, step - 1], h_r.at[h, way, step - 1], *to)

    def ring_arrived(h, way, step):
        arrived(ht.at[ring_slot(way, step), h], h_s.at[0, 0, 0], h_r.at[h, way, step - 1])

    def forward(h, step):
        for way in range(2):
            if step > 1:
                ring_arrived(h, way, step - 1)
            if step < 4 or way == h:
                ring_copy(h, way, step).start()
                leaving.append(ring_copy(h, way, step).wait_send)

    def project(h):
        heads = lax.dot_general(
            pt[:, h].reshape(NY * 16, NZ * LANES),
            cbuf[...].reshape(tokens, NZ * LANES),
            (((1,), (1,)), ((), ())),
            preferred_element_type=jnp.float32,
        )
        ht[y, h] = heads.astype(jnp.bfloat16)

    def product(h, slots, blocks, start):
        left = jnp.concatenate([ht[slot, h] for slot in slots], axis=1)
        for s in blocks:
            right = jnp.concatenate([xbuf[s, :, slot].reshape(tokens, 256) for slot in slots], axis=0)
            part = jnp.dot(left, right, preferred_element_type=jnp.float32)
            acc[h, s] = part if start else acc[h, s] + part

    def rows_copy(i):
        oa, oc = trio_at(i)
        return rdma(
            pt.at[:, :, :, pl.ds(pl.multiple_of((d // 2) * LANES, LANES), LANES)],
            rows.at[c, a],
            rows_s.at[i],
            rows_r.at[own_s],
            d,
            oa * (NY * NC) + y * NC + oc,
        )

    def pass_on(half):
        arrived(xbuf.at[far_s, half], x_s.at[0, 0], x_r.at[far_s, half])
        x_pass(half).start()
        leaving.append(x_pass(half).wait_send)

    loads[1].wait()
    for i in range(3):
        oa, oc = trio_at(i)
        arrived(cbuf.at[oa * NC + oc], c_s.at[0], c_r.at[oa * NC + oc])
    for h in waves:
        for k in order:
            slab_arrived(h, k)
        project(h)
        forward(h, 1)
    for i in range(3):
        rows_copy(i).start()
        leaving.append(rows_copy(i).wait_send)
    rows[c, a] = pt[:, :, :, pl.ds(pl.multiple_of((d // 2) * LANES, LANES), LANES)]
    pass_on(0)
    forward(0, 2)
    forward(1, 2)
    forward(0, 3)
    pass_on(1)
    forward(1, 3)
    sib_s = a * NC + 1 - c
    other_s = (1 - a) * NC + 1 - c
    here, far = (own_s, sib_s), (far_s, other_s)
    near = (y, ring_slot(0, 1), ring_slot(1, 1))
    wide = (ring_slot(0, 2), ring_slot(1, 2), ring_slot(0, 3), ring_slot(1, 3))
    last = (ring_slot(0, 4),)
    loads[0].wait()
    for half in range(NA):
        arrived(xbuf.at[sib_s, half], x_s.at[0, 0], x_r.at[sib_s, half])
    product(0, near, here, True)
    forward(0, 4)
    product(1, near, here, True)
    forward(1, 4)
    for half in range(NA):
        arrived(xbuf.at[other_s, half], x_s.at[0, 0], x_r.at[other_s, half])

    def r_copy(h, k):
        to = (z + k) % NZ
        return rdma(rsend.at[h, to], rrecv.at[h, z], r_s.at[h, k], r_r.at[h, z], b * NZ + to, f)

    for h in waves:
        product(h, near, far, True)
        product(h, wide, here + far, False)
        ring_arrived(h, h, 4)
        product(h, last, here + far, False)
        for s in range(NA * NC):
            rsend[h, :, s] = acc[h, s].astype(jnp.bfloat16).reshape(NZ, 16, 256)
        for k in order:
            r_copy(h, k).start()
            leaving.append(r_copy(h, k).wait_send)

    for i in range(3):
        oa, oc = trio_at(i)
        arrived(rows.at[oc, oa], rows_s.at[0], rows_r.at[oa * NC + oc])
    for m in range(MATS):
        rows_t[m] = rows[m].reshape(512, LANES).T
    loads[2].wait()
    loads[3].wait()

    def f_self(s):
        return jnp.logical_and(s == own_s, a == b)

    def f_copy(h, s):
        return rdma(
            fsend.at[h, s],
            frecv.at[h, b, c],
            f_s.at[h, s],
            f_r.at[h, b * NC + c],
            a * NZ + z,
            (s // NC) * (NY * NC) + y * NC + s % NC,
        )

    def d_copy(h, k):
        to = along_z(k) if k else ((1 - b) * NZ + z, f)
        return rdma(dirs.at[d, h], dirs.at[d, h], d_s.at[h, k], d_r.at[h, d], *to)

    def d_pass(h, k):
        piece = dirs.at[b * NZ + (z + k) % NZ, h]
        return rdma(
            piece, piece, p_s.at[h, k], d_r.at[h, b * NZ + (z + k) % NZ], (1 - b) * NZ + z, f
        )

    inverse_root = 1.0 / math.sqrt(TOKENS)
    for h in waves:
        total = rsend[h, z].astype(jnp.float32)
        for k in order:
            source = (z + k) % NZ
            arrived(rrecv.at[h, source], r_s.at[0, 0], r_r.at[h, source])
            total = total + rrecv[h, source].astype(jnp.float32)
        fsend[h] = total.astype(jnp.bfloat16)
        for s in range(NA * NC):

            @pl.when(jnp.logical_not(f_self(s)))
            def _(h=h, s=s):
                f_copy(h, s).start()

            @pl.when(f_self(s))
            def _(h=h, s=s):
                pltpu.make_async_copy(fsend.at[h, s], frecv.at[h, b, c], f_r.at[h, b * NC + c]).start()

        for k in range(NB):
            for m in range(NC):
                arrived(frecv.at[h, k, m], f_s.at[0, 0], f_r.at[h, k * NC + m])
        block = slice(16 * h, 16 * h + 16)
        projected = (frecv[h, 0].astype(jnp.float32) + frecv[h, 1].astype(jnp.float32)) * inverse_root
        first = beta_first * first_in[:, block] + (1.0 - beta_first) * projected
        second = beta_second * second_in[:, block] + (1.0 - beta_second) * projected * projected
        direction = (
            first / (1.0 - beta_first**STEP) / (jnp.sqrt(second / (1.0 - beta_second**STEP)) + epsilon)
        )
        dirs[d, h] = direction.astype(jnp.bfloat16)
        for k in (0,) + order:
            d_copy(h, k).start()
            leaving.append(d_copy(h, k).wait_send)
        first_out[:, block] = first
        second_out[:, block] = second

    def f_left():
        for h in waves:
            for s in range(NA * NC):

                @pl.when(jnp.logical_not(f_self(s)))
                def _(h=h, s=s):
                    f_copy(h, s).wait_send()

    leaving.append(f_left)

    for h in waves:
        for k in order:
            source = b * NZ + (z + k) % NZ
            arrived(dirs.at[source, h], d_s.at[0, 0], d_r.at[h, source])
            d_pass(h, k).start()
            leaving.append(d_pass(h, k).wait_send)
    for h in waves:
        for k in (0,) + order:
            source = (1 - b) * NZ + (z + k) % NZ
            arrived(dirs.at[source, h], d_s.at[0, 0], d_r.at[h, source])

    for m in range(MATS):
        update_out[m] = jnp.dot(
            rows_t[m, pl.ds(pl.multiple_of((d % 2) * 64, 64), 64), :],
            dirs[:, :, m].reshape(512, 256),
            preferred_element_type=jnp.float32,
        ).astype(jnp.bfloat16)

    for wait in leaving:
        wait()


def on_device(layer_input, cotangent, candidates, moment_first, moment_second, owners):
    bf16, f32 = jnp.bfloat16, jnp.float32
    x = layer_input.reshape(NA, NY, 128, 256)
    cand = jnp.swapaxes(candidates[:, 0], 1, 2)
    vmem = pl.BlockSpec(memory_space=pltpu.VMEM)
    hbm = pl.BlockSpec(memory_space=pl.ANY)
    sem = pltpu.SemaphoreType.DMA
    return pl.pallas_call(
        kernel,
        out_shape=(
            jax.ShapeDtypeStruct((MATS, 64, 256), bf16),
            jax.ShapeDtypeStruct((MATS, 32, 256), f32),
            jax.ShapeDtypeStruct((MATS, 32, 256), f32),
        ),
        in_specs=[pl.BlockSpec(memory_space=pltpu.SMEM), hbm, hbm, hbm, hbm, hbm],
        out_specs=(vmem, vmem, vmem),
        scratch_shapes=[
            pltpu.VMEM((4, NA, NY, 128, 256), bf16),
            pltpu.VMEM((4, 64, 1024), bf16),
            pltpu.VMEM((16, NC, 16, LANES), bf16),
            pltpu.VMEM((NY, NB, 16, 1024), bf16),
            pltpu.VMEM((NY, 2, 128, 256), bf16),
            pltpu.VMEM((2, 4, 128, 256), f32),
            pltpu.VMEM((2, NZ, 4, 16, 256), bf16),
            pltpu.VMEM((2, NZ, 4, 16, 256), bf16),
            pltpu.VMEM((2, 4, 16, 256), bf16),
            pltpu.VMEM((2, NB, MATS, 16, 256), bf16),
            pltpu.VMEM((16, 2, MATS, 16, 256), bf16),
            pltpu.VMEM((MATS, NA, NY, NB, 16, LANES), bf16),
            pltpu.VMEM((MATS, LANES, 512), bf16),
            pltpu.VMEM((MATS, 32, 256), f32),
            pltpu.VMEM((MATS, 32, 256), f32),
            sem((4,)),
            sem((NA, 3)),
            sem((4, NA)),
            sem((3,)),
            sem((4,)),
            sem((MATS, 16)),
            sem((16, NC)),
            sem((2, NZ)),
            sem((2, NZ)),
            sem((2, NY)),
            sem((2, NY)),
            sem((3,)),
            sem((4,)),
            sem((2, 2, 4)),
            sem((2, 2, 4)),
            sem((2, NZ)),
            sem((2, NZ)),
            sem((2, 4)),
            sem((2, 4)),
            sem((2, NZ)),
            sem((2, 16)),
            sem((2, NZ)),
        ],
        compiler_params=pltpu.CompilerParams(
            collective_id=0, has_side_effects=True, vmem_limit_bytes=67043328
        ),
    )(owners, x, cotangent, cand, moment_first, moment_second)


def solution(mesh):
    placed = (
        P("dp", "fsdp"),
        P(None, ("dp", "fsdp"), None),
        P(None, "dp", None, "fsdp"),
        P(None, "dp", "fsdp"),
        P(None, "dp", "fsdp"),
        P(),
    )
    return jax.shard_map(
        on_device,
        mesh=mesh,
        in_specs=placed,
        out_specs=(P(None, "dp", "fsdp"), P(None, "dp", "fsdp"), P(None, "dp", "fsdp")),
        check_vma=False,
    )
```

```python
import math

import jax
import jax.numpy as jnp
from jax import lax
from jax.experimental import pallas as pl
from jax.experimental.pallas import tpu as pltpu
from jax.sharding import PartitionSpec as P

MATS = 2
STEP = 10
TOKENS = 32768
NB = 2
NZ = 8
NA = 2
NY = 8
NC = 2
LANES = 128

beta_first = 0.9
beta_second = 0.999
epsilon = 1e-08

MESH = pl.DeviceIdType.MESH


def kernel(
    owners,
    x_hbm,
    c_hbm,
    cand,
    first_hbm,
    second_hbm,
    update_out,
    projected_out,
    xbuf,
    cbuf,
    cbuf_t,
    picked,
    pt,
    ht,
    acc,
    bsend,
    brecv,
    rsend,
    rrecv,
    dirs,
    rows,
    rows_t,
    first_in,
    second_in,
    local_sem,
    x_s,
    x_r,
    c_s,
    c_r,
    pick_s,
    pick_r,
    tile_s,
    tile_r,
    slab_s,
    slab_r,
    rows_s,
    rows_r,
    h_s,
    h_r,
    b_s,
    b_r,
    r_s,
    r_r,
    d_s,
    d_r,
    p_s,
):
    d = lax.axis_index("dp")
    f = lax.axis_index("fsdp")
    b, z = d // NZ, d % NZ
    a, y, c = f // (NY * NC), (f // NC) % NY, f % NC
    own_s = a * NC + c

    def rdma(src, dst, send, recv, dp, fsdp):
        return pltpu.make_async_remote_copy(
            src_ref=src, dst_ref=dst, send_sem=send, recv_sem=recv, device_id=(dp, fsdp), device_id_type=MESH
        )

    def arrived(dst, send, recv):
        rdma(dst, dst, send, recv, d, f).wait_recv()

    def sent(src, send, recv):
        rdma(src, src, send, recv, d, f).wait_send()

    barrier = pltpu.get_barrier_semaphore()
    leaving = []

    def greet(dp, fsdp):
        pl.semaphore_signal(barrier, inc=1, device_id=(dp, fsdp), device_id_type=MESH)

    @pl.loop(0, NB * NZ)
    def _(k):
        for core in range(NC):

            @pl.when(jnp.logical_or(k != d, core != c))
            def _():
                greet(k, a * (NY * NC) + y * NC + core)

    for k in range(NB):
        for core in range(NC):
            greet(k * NZ + z, (1 - a) * (NY * NC) + y * NC + core)
    for k in range(1, NY):
        greet(d, a * (NY * NC) + ((y + k) % NY) * NC + c)

    loads = [
        pltpu.make_async_copy(x_hbm, xbuf.at[own_s], local_sem.at[0]),
        pltpu.make_async_copy(c_hbm.at[c], cbuf.at[own_s], local_sem.at[1]),
        pltpu.make_async_copy(first_hbm, first_in, local_sem.at[2]),
        pltpu.make_async_copy(second_hbm, second_in, local_sem.at[3]),
    ]
    for load in loads:
        load.start()
    pl.semaphore_wait(barrier, NB * NZ * NC - 1 + NB * NC + NY - 1)

    def pick_copy(m, k):
        return rdma(
            cand.at[m, :, pl.ds(pl.multiple_of((k % NZ) * LANES, LANES), LANES)],
            picked.at[d, c],
            pick_s.at[m, k],
            pick_r.at[d, c],
            k,
            a * (NY * NC) + y * NC + m,
        )

    def pick_self(m, k):
        return jnp.logical_and(c == m, k == d)

    for m in range(MATS):

        @pl.loop(0, NB * NZ)
        def _(k, m=m):
            @pl.when(jnp.logical_not(pick_self(m, k)))
            def _():
                pick_copy(m, k).start()

    lanes_own = pl.ds(pl.multiple_of(z * LANES, LANES), LANES)
    pick_own = pltpu.make_async_copy(cand.at[c, :, lanes_own], picked.at[d, c], pick_r.at[d, c])
    pick_own.start()

    def picks_left():
        for m in range(MATS):

            @pl.loop(0, NB * NZ)
            def _(k, m=m):
                @pl.when(jnp.logical_not(pick_self(m, k)))
                def _():
                    pick_copy(m, k).wait_send()

    leaving.append(picks_left)

    trio = ((0, 1), (1, 0), (1, 1))

    def trio_at(i):
        da, dc = trio[i]
        return (a + da) % NA, (c + dc) % NC

    def c_copy(i):
        oa, oc = trio_at(i)
        return rdma(c_hbm.at[oc], cbuf.at[own_s], c_s.at[i], c_r.at[own_s], d, oa * (NY * NC) + y * NC + oc)

    def x_copy(half, away):
        oa, oc = (1 - a, c) if away else (a, 1 - c)
        return rdma(
            x_hbm.at[half],
            xbuf.at[own_s, half],
            x_s.at[half, away],
            x_r.at[own_s, half],
            d,
            oa * (NY * NC) + y * NC + oc,
        )

    far_s = (1 - a) * NC + c

    def x_pass(half):
        return rdma(
            xbuf.at[far_s, half],
            xbuf.at[far_s, half],
            x_s.at[half, 2],
            x_r.at[far_s, half],
            d,
            a * (NY * NC) + y * NC + 1 - c,
        )

    for i in range(3):
        c_copy(i).start()
        leaving.append(c_copy(i).wait_send)
    for half in range(NA):
        x_copy(half, 1).start()
        leaving.append(x_copy(half, 1).wait_send)
    for half in range(NA):
        x_copy(half, 0).start()
        leaving.append(x_copy(half, 0).wait_send)

    for core in range(NC):

        @pl.loop(0, NB * NZ)
        def _(k, core=core):
            arrived(picked.at[k, core], pick_s.at[0, 0], pick_r.at[k, core])

    pt[y, :, :, lanes_own] = picked[owners[c]]
    order = (4, 3, 5, 2, 6, 1, 7)
    waves = range(2)

    def along_y(k):
        return d, a * (NY * NC) + ((y + k) % NY) * NC + c

    def along_z(k):
        return b * NZ + (z + k) % NZ, f

    def tile_copy(h, k):
        tile = pt.at[y, h, :, lanes_own]
        to = along_y(k) if h else along_z(k)
        return rdma(tile, tile, tile_s.at[h, k], tile_r.at[h, y if h else z], *to)

    def tile_arrived(h, k):
        source = ((y if h else z) + k) % NZ
        lanes = lanes_own if h else pl.ds(pl.multiple_of(source * LANES, LANES), LANES)
        arrived(pt.at[source if h else y, h, :, lanes], tile_s.at[0, 0], tile_r.at[h, source])

    def slab_copy(h, k):
        slab = pt.at[:, h, :, lanes_own] if h else pt.at[y, h]
        to = along_z(k) if h else along_y(k)
        return rdma(slab, slab, slab_s.at[h, k], slab_r.at[h, z if h else y], *to)

    def slab_arrived(h, k):
        source = ((z if h else y) + k) % NZ
        lanes = pl.ds(pl.multiple_of(source * LANES, LANES), LANES)
        arrived(pt.at[:, h, :, lanes] if h else pt.at[source, h], slab_s.at[0, 0], slab_r.at[h, source])

    for h in waves:
        for k in order:
            tile_copy(h, k).start()
            leaving.append(tile_copy(h, k).wait_send)
    for h in waves:
        for k in order:
            tile_arrived(h, k)
        for k in order:
            slab_copy(h, k).start()
            leaving.append(slab_copy(h, k).wait_send)

    tokens = NA * NC * cbuf.shape[1]

    def ring_slot(way, step):
        return (y - step + NY) % NY if way == 0 else (y + step) % NY

    def ring_copy(h, way, step):
        piece = ht.at[ring_slot(way, step - 1), h]
        to = along_y(1 if way == 0 else NY - 1)
        return rdma(piece, piece, h_s.at[h, way, step - 1], h_r.at[h, way, step - 1], *to)

    def ring_arrived(h, way, step):
        arrived(ht.at[ring_slot(way, step), h], h_s.at[0, 0, 0], h_r.at[h, way, step - 1])

    def forward(h, step):
        for way in range(2):
            if step > 1:
                ring_arrived(h, way, step - 1)
            if step < 4 or way == h:
                ring_copy(h, way, step).start()
                leaving.append(ring_copy(h, way, step).wait_send)

    def project(h):
        heads = lax.dot_general(
            pt[:, h].reshape(NY * 16, NZ * LANES),
            cbuf_t[...],
            (((1,), (0,)), ((), ())),
            preferred_element_type=jnp.float32,
        )
        ht[y, h] = heads.astype(jnp.bfloat16)

    def product(h, slots, blocks, start):
        left = jnp.concatenate([ht[slot, h] for slot in slots], axis=1)
        for s in blocks:
            right = jnp.concatenate([xbuf[s, :, slot].reshape(tokens, 256) for slot in slots], axis=0)
            part = jnp.dot(left, right, preferred_element_type=jnp.float32)
            acc[h, s] = part if start else acc[h, s] + part

    def rows_copy(i):
        oa, oc = trio_at(i)
        return rdma(
            pt.at[:, :, :, pl.ds(pl.multiple_of((d // 2) * LANES, LANES), LANES)],
            rows.at[c, a],
            rows_s.at[i],
            rows_r.at[own_s],
            d,
            oa * (NY * NC) + y * NC + oc,
        )

    def pass_on(half):
        arrived(xbuf.at[far_s, half], x_s.at[0, 0], x_r.at[far_s, half])
        x_pass(half).start()
        leaving.append(x_pass(half).wait_send)

    loads[1].wait()
    for i in range(3):
        oa, oc = trio_at(i)
        arrived(cbuf.at[oa * NC + oc], c_s.at[0], c_r.at[oa * NC + oc])
    cbuf_t[...] = cbuf[...].reshape(tokens, NZ * LANES).T
    for h in waves:
        for k in order:
            slab_arrived(h, k)
        project(h)
        forward(h, 1)
    for i in range(3):
        rows_copy(i).start()
        leaving.append(rows_copy(i).wait_send)
    rows[c, a] = pt[:, :, :, pl.ds(pl.multiple_of((d // 2) * LANES, LANES), LANES)]
    pass_on(0)
    forward(0, 2)
    forward(1, 2)
    forward(0, 3)
    forward(1, 3)
    pass_on(1)
    sib_s = a * NC + 1 - c
    other_s = (1 - a) * NC + 1 - c
    here, far = (own_s, sib_s), (far_s, other_s)
    near = (y, ring_slot(0, 1), ring_slot(1, 1))
    wide = (ring_slot(0, 2), ring_slot(1, 2), ring_slot(0, 3), ring_slot(1, 3))
    last = (ring_slot(0, 4),)
    loads[0].wait()
    for half in range(NA):
        arrived(xbuf.at[sib_s, half], x_s.at[0, 0], x_r.at[sib_s, half])
    product(0, near, here, True)
    forward(0, 4)
    product(1, near, here, True)
    forward(1, 4)
    for half in range(NA):
        arrived(xbuf.at[other_s, half], x_s.at[0, 0], x_r.at[other_s, half])

    def b_copy(h, k):
        to = (z + k) % NZ
        return rdma(
            bsend.at[h, to], brecv.at[h, to], b_s.at[h, k], b_r.at[h, to], (1 - b) * NZ + z, f
        )

    def r_copy(h, k, core):
        to = (z + k) % NZ
        return rdma(
            rsend.at[h, to, core],
            rrecv.at[h, c, z],
            r_s.at[h, k, core],
            r_r.at[h, c, z],
            a * NZ + to,
            b * (NY * NC) + y * NC + core,
        )

    def r_self(core):
        return jnp.logical_and(core == c, a == b)

    for h in waves:
        product(h, near, far, True)
        product(h, wide, here + far, False)
    for h in waves:
        ring_arrived(h, h, 4)
        product(h, last, here + far, False)
        for core in range(NC):
            bsend[h, :, core] = acc[h, (1 - b) * NC + core].astype(jnp.bfloat16).reshape(NZ, 16, 256)
        for k in order + (0,):
            b_copy(h, k).start()
            leaving.append(b_copy(h, k).wait_send)

    def both(h, to):
        arrived(brecv.at[h, to], b_s.at[0, 0], b_r.at[h, to])
        mine = [acc[h, b * NC + core, pl.ds(pl.multiple_of(to * 16, 16), 16), :] for core in range(NC)]
        return jnp.stack(mine) + brecv[h, to].astype(jnp.float32)

    for h in waves:
        for k in order + (0,):
            rsend[h, (z + k) % NZ] = both(h, (z + k) % NZ).astype(jnp.bfloat16)
            for core in range(NC):
                if k:
                    r_copy(h, k, core).start()
                    leaving.append(r_copy(h, k, core).wait_send)
                else:

                    @pl.when(jnp.logical_not(r_self(core)))
                    def _(h=h, core=core):
                        r_copy(h, 0, core).start()

                    @pl.when(r_self(core))
                    def _(h=h, core=core):
                        pltpu.make_async_copy(rsend.at[h, z, core], rrecv.at[h, c, z], r_r.at[h, c, z]).start()

    def r_left():
        for h in waves:
            for core in range(NC):

                @pl.when(jnp.logical_not(r_self(core)))
                def _(h=h, core=core):
                    r_copy(h, 0, core).wait_send()

    leaving.append(r_left)
    for i in range(3):
        oa, oc = trio_at(i)
        arrived(rows.at[oc, oa], rows_s.at[0], rows_r.at[oa * NC + oc])
    for m in range(MATS):
        for h in waves:
            rows_t[m, h] = rows[m, :, :, h].reshape(256, LANES).T
    loads[2].wait()
    loads[3].wait()

    def d_copy(h, k):
        to = along_z(k) if k else ((1 - b) * NZ + z, f)
        return rdma(dirs.at[d, h], dirs.at[d, h], d_s.at[h, k], d_r.at[h, d], *to)

    def d_pass(h, k):
        piece = dirs.at[b * NZ + (z + k) % NZ, h]
        return rdma(
            piece, piece, p_s.at[h, k], d_r.at[h, b * NZ + (z + k) % NZ], (1 - b) * NZ + z, f
        )

    inverse_root = 1.0 / math.sqrt(TOKENS)
    for h in waves:
        for k in (0,) + order:
            for m in range(MATS):
                arrived(rrecv.at[h, m, (z + k) % NZ], r_s.at[0, 0, 0], r_r.at[h, m, (z + k) % NZ])
        block = slice(16 * h, 16 * h + 16)
        projected = jnp.sum(rrecv[h].astype(jnp.float32), axis=1) * inverse_root
        first = beta_first * first_in[:, block] + (1.0 - beta_first) * projected
        second = beta_second * second_in[:, block] + (1.0 - beta_second) * projected * projected
        direction = (
            first / (1.0 - beta_first**STEP) / (jnp.sqrt(second / (1.0 - beta_second**STEP)) + epsilon)
        )
        dirs[d, h] = direction.astype(jnp.bfloat16)
        for k in (0,) + order:
            d_copy(h, k).start()
            leaving.append(d_copy(h, k).wait_send)
        projected_out[:, block] = projected

    for h in waves:
        for k in order:
            source = b * NZ + (z + k) % NZ
            arrived(dirs.at[source, h], d_s.at[0, 0], d_r.at[h, source])
            d_pass(h, k).start()
            leaving.append(d_pass(h, k).wait_send)
    updates = []
    own_rows = pl.ds(pl.multiple_of((d % 2) * 64, 64), 64)
    for h in waves:
        for k in (0,) + order:
            source = (1 - b) * NZ + (z + k) % NZ
            arrived(dirs.at[source, h], d_s.at[0, 0], d_r.at[h, source])
        updates.append(
            [
                jnp.dot(
                    rows_t[m, h, own_rows, :],
                    dirs[:, h, m].reshape(256, 256),
                    preferred_element_type=jnp.float32,
                )
                for m in range(MATS)
            ]
        )
    for m in range(MATS):
        update_out[m] = updates[0][m] + updates[1][m]

    for wait in leaving:
        wait()


def on_device(layer_input, cotangent, candidates, moment_first, moment_second, owners):
    bf16, f32 = jnp.bfloat16, jnp.float32
    x = layer_input.reshape(NA, NY, 128, 256)
    cand = jnp.swapaxes(candidates[:, 0], 1, 2)
    vmem = pl.BlockSpec(memory_space=pltpu.VMEM)
    hbm = pl.BlockSpec(memory_space=pl.ANY)
    sem = pltpu.SemaphoreType.DMA
    update, projected = pl.pallas_call(
        kernel,
        out_shape=(
            jax.ShapeDtypeStruct((MATS, 64, 256), f32),
            jax.ShapeDtypeStruct((MATS, 32, 256), f32),
        ),
        in_specs=[pl.BlockSpec(memory_space=pltpu.SMEM), hbm, hbm, hbm, hbm, hbm],
        out_specs=(vmem, vmem),
        scratch_shapes=[
            pltpu.VMEM((4, NA, NY, 128, 256), bf16),
            pltpu.VMEM((4, 64, 1024), bf16),
            pltpu.VMEM((1024, 256), bf16),
            pltpu.VMEM((16, NC, 16, LANES), bf16),
            pltpu.VMEM((NY, NB, 16, 1024), bf16),
            pltpu.VMEM((NY, 2, 128, 256), bf16),
            pltpu.VMEM((2, 4, 128, 256), f32),
            pltpu.VMEM((2, NZ, NC, 16, 256), bf16),
            pltpu.VMEM((2, NZ, NC, 16, 256), bf16),
            pltpu.VMEM((2, NZ, NC, 16, 256), bf16),
            pltpu.VMEM((2, MATS, NZ, 16, 256), bf16),
            pltpu.VMEM((16, 2, MATS, 16, 256), bf16),
            pltpu.VMEM((MATS, NA, NY, NB, 16, LANES), bf16),
            pltpu.VMEM((MATS, 2, LANES, 256), bf16),
            pltpu.VMEM((MATS, 32, 256), f32),
            pltpu.VMEM((MATS, 32, 256), f32),
            sem((4,)),
            sem((NA, 3)),
            sem((4, NA)),
            sem((3,)),
            sem((4,)),
            sem((MATS, 16)),
            sem((16, NC)),
            sem((2, NZ)),
            sem((2, NZ)),
            sem((2, NY)),
            sem((2, NY)),
            sem((3,)),
            sem((4,)),
            sem((2, 2, 4)),
            sem((2, 2, 4)),
            sem((2, NZ)),
            sem((2, NZ)),
            sem((2, NZ, NC)),
            sem((2, MATS, NZ)),
            sem((2, NZ)),
            sem((2, 16)),
            sem((2, NZ)),
        ],
        compiler_params=pltpu.CompilerParams(
            collective_id=0, has_side_effects=True, vmem_limit_bytes=67043328
        ),
    )(owners, x, cotangent, cand, moment_first, moment_second)
    first = beta_first * moment_first + (1.0 - beta_first) * projected
    second = beta_second * moment_second + (1.0 - beta_second) * projected * projected
    return update.astype(bf16), first, second


def solution(mesh):
    placed = (
        P("dp", "fsdp"),
        P(None, ("dp", "fsdp"), None),
        P(None, "dp", None, "fsdp"),
        P(None, "dp", "fsdp"),
        P(None, "dp", "fsdp"),
        P(),
    )
    return jax.shard_map(
        on_device,
        mesh=mesh,
        in_specs=placed,
        out_specs=(P(None, "dp", "fsdp"), P(None, "dp", "fsdp"), P(None, "dp", "fsdp")),
        check_vma=False,
    )
```

```python
import math

import jax
import jax.numpy as jnp
from jax import lax
from jax.experimental import pallas as pl
from jax.experimental.pallas import tpu as pltpu
from jax.sharding import PartitionSpec as P

MATS = 2
STEP = 10
TOKENS = 32768
NB = 2
NZ = 8
NA = 2
NY = 8
NC = 2
LANES = 128

beta_first = 0.9
beta_second = 0.999
epsilon = 1e-08

MESH = pl.DeviceIdType.MESH


def kernel(
    owners_hbm,
    x_hbm,
    c_hbm,
    cand,
    first_hbm,
    second_hbm,
    update_out,
    projected_out,
    xbuf,
    cbuf,
    cbuf_t,
    picked,
    pt,
    qt,
    ht,
    acc,
    bsend,
    brecv,
    rsend,
    rrecv,
    dirs,
    rows,
    rows_t,
    first_in,
    second_in,
    owners,
    local_sem,
    x_s,
    x_r,
    c_s,
    c_r,
    pick_s,
    pick_r,
    tile_s,
    tile_r,
    slab_s,
    slab_r,
    rows_s,
    rows_r,
    h_s,
    h_r,
    b_s,
    b_r,
    r_s,
    r_r,
    d_s,
    d_r,
    p_s,
):
    d = lax.axis_index("dp")
    f = lax.axis_index("fsdp")
    b, z = d // NZ, d % NZ
    a, y, c = f // (NY * NC), (f // NC) % NY, f % NC
    own_s = a * NC + c

    def rdma(src, dst, send, recv, dp, fsdp):
        return pltpu.make_async_remote_copy(
            src_ref=src, dst_ref=dst, send_sem=send, recv_sem=recv, device_id=(dp, fsdp), device_id_type=MESH
        )

    def arrived(dst, send, recv):
        rdma(dst, dst, send, recv, d, f).wait_recv()

    def sent(src, send, recv):
        rdma(src, src, send, recv, d, f).wait_send()

    barrier = pltpu.get_barrier_semaphore()
    leaving = []

    def greet(dp, fsdp):
        pl.semaphore_signal(barrier, inc=1, device_id=(dp, fsdp), device_id_type=MESH)

    @pl.loop(0, NB * NZ)
    def _(k):
        for core in range(NC):

            @pl.when(jnp.logical_or(k != d, core != c))
            def _():
                greet(k, a * (NY * NC) + y * NC + core)

    for k in range(NB):
        for core in range(NC):
            greet(k * NZ + z, (1 - a) * (NY * NC) + y * NC + core)
    for k in range(1, NY):
        greet(d, a * (NY * NC) + ((y + k) % NY) * NC + c)

    owners_load = pltpu.make_async_copy(owners_hbm, owners, local_sem.at[4])
    owners_load.start()
    loads = [
        pltpu.make_async_copy(x_hbm, xbuf.at[own_s], local_sem.at[0]),
        pltpu.make_async_copy(c_hbm.at[c], cbuf.at[own_s], local_sem.at[1]),
        pltpu.make_async_copy(first_hbm, first_in, local_sem.at[2]),
        pltpu.make_async_copy(second_hbm, second_in, local_sem.at[3]),
    ]
    for load in loads:
        load.start()
    pl.semaphore_wait(barrier, NB * NZ * NC - 1 + NB * NC + NY - 1)

    def pick_copy(m, k):
        return rdma(
            cand.at[m, :, pl.ds(pl.multiple_of((k % NZ) * LANES, LANES), LANES)],
            picked.at[d, c],
            pick_s.at[m, k],
            pick_r.at[d, c],
            k,
            a * (NY * NC) + y * NC + m,
        )

    def pick_self(m, k):
        return jnp.logical_and(c == m, k == d)

    for m in range(MATS):

        @pl.loop(0, NB * NZ)
        def _(k, m=m):
            @pl.when(jnp.logical_not(pick_self(m, k)))
            def _():
                pick_copy(m, k).start()

    lanes_own = pl.ds(pl.multiple_of(z * LANES, LANES), LANES)
    pick_own = pltpu.make_async_copy(cand.at[c, :, lanes_own], picked.at[d, c], pick_r.at[d, c])
    pick_own.start()

    def picks_left():
        for m in range(MATS):

            @pl.loop(0, NB * NZ)
            def _(k, m=m):
                @pl.when(jnp.logical_not(pick_self(m, k)))
                def _():
                    pick_copy(m, k).wait_send()

    leaving.append(picks_left)

    trio = ((0, 1), (1, 0), (1, 1))

    def trio_at(i):
        da, dc = trio[i]
        return (a + da) % NA, (c + dc) % NC

    def c_copy(i):
        oa, oc = trio_at(i)
        return rdma(c_hbm.at[oc], cbuf.at[own_s], c_s.at[i], c_r.at[own_s], d, oa * (NY * NC) + y * NC + oc)

    parts = range(4)

    def x_part(ref, part):
        return ref.at[part // 2, pl.ds(part % 2 * 4, 4)]

    def x_copy(half, away):
        oa, oc = (1 - a, c) if away else (a, 1 - c)
        return rdma(
            x_part(x_hbm, half),
            x_part(xbuf.at[own_s], half),
            x_s.at[half, away],
            x_r.at[own_s, half],
            d,
            oa * (NY * NC) + y * NC + oc,
        )

    far_s = (1 - a) * NC + c

    def x_pass(half):
        return rdma(
            x_part(xbuf.at[far_s], half),
            x_part(xbuf.at[far_s], half),
            x_s.at[half, 2],
            x_r.at[far_s, half],
            d,
            a * (NY * NC) + y * NC + 1 - c,
        )

    for i in range(3):
        c_copy(i).start()
        leaving.append(c_copy(i).wait_send)
    for half in parts:
        x_copy(half, 1).start()
        leaving.append(x_copy(half, 1).wait_send)
    for half in parts:
        x_copy(half, 0).start()
        leaving.append(x_copy(half, 0).wait_send)

    for core in range(NC):

        @pl.loop(0, NB * NZ)
        def _(k, core=core):
            arrived(picked.at[k, core], pick_s.at[0, 0], pick_r.at[k, core])

    owners_load.wait()
    chosen = picked[owners[c]]
    pt[y, :, lanes_own] = chosen[0]
    qt[z, y] = chosen[1]
    order = (4, 3, 5, 2, 6, 1, 7)
    waves = range(2)

    def along_y(k):
        return d, a * (NY * NC) + ((y + k) % NY) * NC + c

    def along_z(k):
        return b * NZ + (z + k) % NZ, f

    def lanes_of(k):
        return pl.ds(pl.multiple_of((z + k) % NZ * LANES, LANES), LANES)

    def tile_of(h, k):
        return qt.at[z, (y + k) % NY] if h else pt.at[y, :, lanes_of(k)]

    def tile_copy(h, k):
        to = along_y(k) if h else along_z(k)
        return rdma(tile_of(h, 0), tile_of(h, 0), tile_s.at[h, k], tile_r.at[h, y if h else z], *to)

    def tile_arrived(h, k):
        arrived(tile_of(h, k), tile_s.at[0, 0], tile_r.at[h, ((y if h else z) + k) % NZ])

    def slab_of(h, k):
        return qt.at[(z + k) % NZ] if h else pt.at[(y + k) % NY]

    def slab_copy(h, k):
        to = along_z(k) if h else along_y(k)
        return rdma(slab_of(h, 0), slab_of(h, 0), slab_s.at[h, k], slab_r.at[h, z if h else y], *to)

    def slab_arrived(h, k):
        arrived(slab_of(h, k), slab_s.at[0, 0], slab_r.at[h, ((z if h else y) + k) % NZ])

    for h in waves:
        for k in order:
            tile_copy(h, k).start()
            leaving.append(tile_copy(h, k).wait_send)
    tokens = NA * NC * cbuf.shape[1]
    loads[1].wait()
    for i in range(3):
        oa, oc = trio_at(i)
        arrived(cbuf.at[oa * NC + oc], c_s.at[0], c_r.at[oa * NC + oc])
    cbuf_t[...] = cbuf[...].reshape(tokens, NZ * LANES).T
    for h in waves:
        for k in order:
            tile_arrived(h, k)
        for k in order:
            slab_copy(h, k).start()
            leaving.append(slab_copy(h, k).wait_send)

    def ring_slot(way, step):
        return (y - step + NY) % NY if way == 0 else (y + step) % NY

    def ring_copy(h, way, step):
        piece = ht.at[ring_slot(way, step - 1), h]
        to = along_y(1 if way == 0 else NY - 1)
        return rdma(piece, piece, h_s.at[h, way, step - 1], h_r.at[h, way, step - 1], *to)

    def ring_arrived(h, way, step):
        arrived(ht.at[ring_slot(way, step), h], h_s.at[0, 0, 0], h_r.at[h, way, step - 1])

    def forward(h, step):
        for way in range(2):
            if step > 1:
                ring_arrived(h, way, step - 1)
            if step < 4 or way == h:
                ring_copy(h, way, step).start()
                leaving.append(ring_copy(h, way, step).wait_send)

    def project(h):
        if h == 0:
            left = pt[...].reshape(NY * 16, NZ * LANES)
        else:
            left = jnp.concatenate([qt[k].reshape(NY * 16, LANES) for k in range(NZ)], axis=1)
        heads = jnp.dot(left, cbuf_t[...], preferred_element_type=jnp.float32)
        ht[y, h] = heads.astype(jnp.bfloat16)

    def product(h, slots, blocks, start):
        left = jnp.concatenate([ht[slot, h] for slot in slots], axis=1)
        for s in blocks:
            right = jnp.concatenate([xbuf[s, :, slot].reshape(tokens, 256) for slot in slots], axis=0)
            part = jnp.dot(left, right, preferred_element_type=jnp.float32)
            acc[h, s] = part if start else acc[h, s] + part

    def rows_of(h):
        block = d // 2
        return qt.at[block] if h else pt.at[:, :, pl.ds(pl.multiple_of(block * LANES, LANES), LANES)]

    def rows_copy(h, i):
        oa, oc = trio_at(i)
        return rdma(
            rows_of(h),
            rows.at[c, a, h],
            rows_s.at[h, i],
            rows_r.at[h, own_s],
            d,
            oa * (NY * NC) + y * NC + oc,
        )

    def pass_on(half):
        arrived(x_part(xbuf.at[far_s], half), x_s.at[0, 0], x_r.at[far_s, half])
        x_pass(half).start()
        leaving.append(x_pass(half).wait_send)

    for h in waves:
        for k in order:
            slab_arrived(h, k)
        project(h)
        forward(h, 1)
    for h in waves:
        for i in range(3):
            rows_copy(h, i).start()
            leaving.append(rows_copy(h, i).wait_send)
        rows[c, a, h] = rows_of(h)[...]
    pass_on(0)
    pass_on(1)
    forward(0, 2)
    forward(1, 2)
    forward(0, 3)
    forward(1, 3)
    pass_on(2)
    pass_on(3)
    sib_s = a * NC + 1 - c
    other_s = (1 - a) * NC + 1 - c
    here, far = (own_s, sib_s), (far_s, other_s)
    near = (y, ring_slot(0, 1), ring_slot(1, 1))
    wide = (ring_slot(0, 2), ring_slot(1, 2), ring_slot(0, 3), ring_slot(1, 3))
    last = (ring_slot(0, 4),)
    loads[0].wait()
    for half in parts:
        arrived(x_part(xbuf.at[sib_s], half), x_s.at[0, 0], x_r.at[sib_s, half])
    product(0, near, here, True)
    forward(0, 4)
    product(1, near, here, True)
    forward(1, 4)
    for half in parts:
        arrived(x_part(xbuf.at[other_s], half), x_s.at[0, 0], x_r.at[other_s, half])

    def b_copy(h, k):
        to = (z + k) % NZ
        return rdma(
            bsend.at[h, to], brecv.at[h, to], b_s.at[h, k], b_r.at[h, to], (1 - b) * NZ + z, f
        )

    def r_copy(h, k, core):
        to = (z + k) % NZ
        return rdma(
            rsend.at[h, to, core],
            rrecv.at[h, c, z],
            r_s.at[h, k, core],
            r_r.at[h, c, z],
            a * NZ + to,
            b * (NY * NC) + y * NC + core,
        )

    def r_self(core):
        return jnp.logical_and(core == c, a == b)

    for h in waves:
        product(h, near, far, True)
        product(h, wide, here + far, False)
    for h in waves:
        ring_arrived(h, h, 4)
        product(h, last, here + far, False)
        for core in range(NC):
            bsend[h, :, core] = acc[h, (1 - b) * NC + core].astype(jnp.bfloat16).reshape(NZ, 16, 256)
        for k in order + (0,):
            b_copy(h, k).start()
            leaving.append(b_copy(h, k).wait_send)

    def both(h, to):
        arrived(brecv.at[h, to], b_s.at[0, 0], b_r.at[h, to])
        mine = [acc[h, b * NC + core, pl.ds(pl.multiple_of(to * 16, 16), 16), :] for core in range(NC)]
        return jnp.stack(mine) + brecv[h, to].astype(jnp.float32)

    for h in waves:
        for k in order + (0,):
            rsend[h, (z + k) % NZ] = both(h, (z + k) % NZ).astype(jnp.bfloat16)
            for core in range(NC):
                if k:
                    r_copy(h, k, core).start()
                    leaving.append(r_copy(h, k, core).wait_send)
                else:

                    @pl.when(jnp.logical_not(r_self(core)))
                    def _(h=h, core=core):
                        r_copy(h, 0, core).start()

                    @pl.when(r_self(core))
                    def _(h=h, core=core):
                        pltpu.make_async_copy(rsend.at[h, z, core], rrecv.at[h, c, z], r_r.at[h, c, z]).start()

    def r_left():
        for h in waves:
            for core in range(NC):

                @pl.when(jnp.logical_not(r_self(core)))
                def _(h=h, core=core):
                    r_copy(h, 0, core).wait_send()

    leaving.append(r_left)
    for i in range(3):
        oa, oc = trio_at(i)
        for h in waves:
            arrived(rows.at[oc, oa, h], rows_s.at[0, 0], rows_r.at[h, oa * NC + oc])
    for m in range(MATS):
        for h in waves:
            rows_t[m, h] = rows[m, :, h].reshape(256, LANES).T
    loads[2].wait()
    loads[3].wait()

    def d_copy(h, k):
        to = along_z(k) if k else ((1 - b) * NZ + z, f)
        return rdma(dirs.at[d, h], dirs.at[d, h], d_s.at[h, k], d_r.at[h, d], *to)

    def d_pass(h, k):
        piece = dirs.at[b * NZ + (z + k) % NZ, h]
        return rdma(
            piece, piece, p_s.at[h, k], d_r.at[h, b * NZ + (z + k) % NZ], (1 - b) * NZ + z, f
        )

    inverse_root = 1.0 / math.sqrt(TOKENS)
    for h in waves:
        for k in (0,) + order:
            for m in range(MATS):
                arrived(rrecv.at[h, m, (z + k) % NZ], r_s.at[0, 0, 0], r_r.at[h, m, (z + k) % NZ])
        block = slice(16 * h, 16 * h + 16)
        projected = jnp.sum(rrecv[h].astype(jnp.float32), axis=1) * inverse_root
        first = beta_first * first_in[:, block] + (1.0 - beta_first) * projected
        second = beta_second * second_in[:, block] + (1.0 - beta_second) * projected * projected
        direction = (
            first / (1.0 - beta_first**STEP) / (jnp.sqrt(second / (1.0 - beta_second**STEP)) + epsilon)
        )
        dirs[d, h] = direction.astype(jnp.bfloat16)
        for k in (0,) + order:
            d_copy(h, k).start()
            leaving.append(d_copy(h, k).wait_send)
        projected_out[:, block] = projected

    for wait in leaving[: len(leaving) - 2 * NZ]:
        wait()
    del leaving[: len(leaving) - 2 * NZ]
    for h in waves:
        for k in order:
            source = b * NZ + (z + k) % NZ
            arrived(dirs.at[source, h], d_s.at[0, 0], d_r.at[h, source])
            d_pass(h, k).start()
            leaving.append(d_pass(h, k).wait_send)
    updates = []
    own_rows = pl.ds(pl.multiple_of((d % 2) * 64, 64), 64)
    for h in waves:
        for k in (0,) + order:
            source = (1 - b) * NZ + (z + k) % NZ
            arrived(dirs.at[source, h], d_s.at[0, 0], d_r.at[h, source])
        updates.append(
            [
                jnp.dot(
                    rows_t[m, h, own_rows, :],
                    dirs[:, h, m].reshape(256, 256),
                    preferred_element_type=jnp.float32,
                )
                for m in range(MATS)
            ]
        )
    for m in range(MATS):
        update_out[m] = updates[0][m] + updates[1][m]

    for wait in leaving:
        wait()


def on_device(layer_input, cotangent, candidates, moment_first, moment_second, owners):
    bf16, f32 = jnp.bfloat16, jnp.float32
    x = layer_input.reshape(NA, NY, 128, 256)
    cand = jnp.swapaxes(candidates[:, 0], 1, 2)
    vmem = pl.BlockSpec(memory_space=pltpu.VMEM)
    hbm = pl.BlockSpec(memory_space=pl.ANY)
    sem = pltpu.SemaphoreType.DMA
    update, projected = pl.pallas_call(
        kernel,
        out_shape=(
            jax.ShapeDtypeStruct((MATS, 64, 256), f32),
            jax.ShapeDtypeStruct((MATS, 32, 256), f32),
        ),
        in_specs=[hbm] * 6,
        out_specs=(vmem, vmem),
        scratch_shapes=[
            pltpu.VMEM((4, NA, NY, 128, 256), bf16),
            pltpu.VMEM((4, 64, 1024), bf16),
            pltpu.VMEM((1024, 256), bf16),
            pltpu.VMEM((16, NC, 16, LANES), bf16),
            pltpu.VMEM((NY, 16, 1024), bf16),
            pltpu.VMEM((NZ, NY, 16, LANES), bf16),
            pltpu.VMEM((NY, 2, 128, 256), bf16),
            pltpu.VMEM((2, 4, 128, 256), f32),
            pltpu.VMEM((2, NZ, NC, 16, 256), bf16),
            pltpu.VMEM((2, NZ, NC, 16, 256), bf16),
            pltpu.VMEM((2, NZ, NC, 16, 256), bf16),
            pltpu.VMEM((2, MATS, NZ, 16, 256), bf16),
            pltpu.VMEM((16, 2, MATS, 16, 256), bf16),
            pltpu.VMEM((MATS, NA, 2, NY, 16, LANES), bf16),
            pltpu.VMEM((MATS, 2, LANES, 256), bf16),
            pltpu.VMEM((MATS, 32, 256), f32),
            pltpu.VMEM((MATS, 32, 256), f32),
            pltpu.SMEM((MATS,), jnp.int32),
            sem((5,)),
            sem((4, 3)),
            sem((4, 4)),
            sem((3,)),
            sem((4,)),
            sem((MATS, 16)),
            sem((16, NC)),
            sem((2, NZ)),
            sem((2, NZ)),
            sem((2, NY)),
            sem((2, NY)),
            sem((2, 3)),
            sem((2, 4)),
            sem((2, 2, 4)),
            sem((2, 2, 4)),
            sem((2, NZ)),
            sem((2, NZ)),
            sem((2, NZ, NC)),
            sem((2, MATS, NZ)),
            sem((2, NZ)),
            sem((2, 16)),
            sem((2, NZ)),
        ],
        compiler_params=pltpu.CompilerParams(
            collective_id=0, has_side_effects=True, vmem_limit_bytes=67043328
        ),
    )(owners, x, cotangent, cand, moment_first, moment_second)
    first = beta_first * moment_first + (1.0 - beta_first) * projected
    second = beta_second * moment_second + (1.0 - beta_second) * projected * projected
    return update.astype(bf16), first, second


def solution(mesh):
    placed = (
        P("dp", "fsdp"),
        P(None, ("dp", "fsdp"), None),
        P(None, "dp", None, "fsdp"),
        P(None, "dp", "fsdp"),
        P(None, "dp", "fsdp"),
        P(),
    )
    return jax.shard_map(
        on_device,
        mesh=mesh,
        in_specs=placed,
        out_specs=(P(None, "dp", "fsdp"), P(None, "dp", "fsdp"), P(None, "dp", "fsdp")),
        check_vma=False,
    )
```

```python
import math

import jax
import jax.numpy as jnp
from jax import lax
from jax.experimental import pallas as pl
from jax.experimental.pallas import tpu as pltpu
from jax.sharding import PartitionSpec as P

MATS = 2
STEP = 10
TOKENS = 32768
NB = 2
NZ = 8
NA = 2
NY = 8
NC = 2
LANES = 128

beta_first = 0.9
beta_second = 0.999
epsilon = 1e-08

MESH = pl.DeviceIdType.MESH


def kernel(
    owners_hbm,
    x_hbm,
    c_hbm,
    cand,
    first_hbm,
    second_hbm,
    update_out,
    projected_out,
    xbuf,
    cbuf,
    cbuf_t,
    picked,
    pt,
    qt,
    ht,
    acc,
    bsend,
    brecv,
    rsend,
    rrecv,
    dirs,
    rows,
    rows_t,
    first_in,
    second_in,
    owners,
    local_sem,
    x_s,
    x_r,
    c_s,
    c_r,
    pick_s,
    pick_r,
    tile_s,
    tile_r,
    slab_s,
    slab_r,
    rows_s,
    rows_r,
    h_s,
    h_r,
    b_s,
    b_r,
    r_s,
    r_r,
    d_s,
    d_r,
    p_s,
):
    d = lax.axis_index("dp")
    f = lax.axis_index("fsdp")
    b, z = d // NZ, d % NZ
    a, y, c = f // (NY * NC), (f // NC) % NY, f % NC
    own_s = a * NC + c

    def rdma(src, dst, send, recv, dp, fsdp):
        return pltpu.make_async_remote_copy(
            src_ref=src, dst_ref=dst, send_sem=send, recv_sem=recv, device_id=(dp, fsdp), device_id_type=MESH
        )

    def arrived(dst, send, recv):
        rdma(dst, dst, send, recv, d, f).wait_recv()

    def sent(src, send, recv):
        rdma(src, src, send, recv, d, f).wait_send()

    barrier = pltpu.get_barrier_semaphore()
    leaving = []

    def greet(dp, fsdp):
        pl.semaphore_signal(barrier, inc=1, device_id=(dp, fsdp), device_id_type=MESH)

    @pl.loop(0, NB * NZ)
    def _(k):
        for core in range(NC):

            @pl.when(jnp.logical_or(k != d, core != c))
            def _():
                greet(k, a * (NY * NC) + y * NC + core)

    for k in range(NB):
        for core in range(NC):
            greet(k * NZ + z, (1 - a) * (NY * NC) + y * NC + core)
    for k in range(1, NY):
        greet(d, a * (NY * NC) + ((y + k) % NY) * NC + c)

    owners_load = pltpu.make_async_copy(owners_hbm, owners, local_sem.at[4])
    owners_load.start()
    loads = [
        pltpu.make_async_copy(x_hbm, xbuf.at[own_s], local_sem.at[0]),
        pltpu.make_async_copy(c_hbm.at[c], cbuf.at[own_s], local_sem.at[1]),
        pltpu.make_async_copy(first_hbm, first_in, local_sem.at[2]),
        pltpu.make_async_copy(second_hbm, second_in, local_sem.at[3]),
    ]
    for load in loads:
        load.start()
    pl.semaphore_wait(barrier, NB * NZ * NC - 1 + NB * NC + NY - 1)

    def pick_copy(m, k):
        return rdma(
            cand.at[m, :, pl.ds(pl.multiple_of((k % NZ) * LANES, LANES), LANES)],
            picked.at[d, c],
            pick_s.at[m, k],
            pick_r.at[d, c],
            k,
            a * (NY * NC) + y * NC + m,
        )

    def pick_self(m, k):
        return jnp.logical_and(c == m, k == d)

    for m in range(MATS):

        @pl.loop(0, NB * NZ)
        def _(k, m=m):
            to = (d + NZ // 2 + k) % (NB * NZ)

            @pl.when(jnp.logical_not(pick_self(m, to)))
            def _():
                pick_copy(m, to).start()

    lanes_own = pl.ds(pl.multiple_of(z * LANES, LANES), LANES)
    pick_own = pltpu.make_async_copy(cand.at[c, :, lanes_own], picked.at[d, c], pick_r.at[d, c])
    pick_own.start()

    def picks_left():
        for m in range(MATS):

            @pl.loop(0, NB * NZ)
            def _(k, m=m):
                @pl.when(jnp.logical_not(pick_self(m, k)))
                def _():
                    pick_copy(m, k).wait_send()

    leaving.append(picks_left)

    trio = ((0, 1), (1, 0), (1, 1))

    def trio_at(i):
        da, dc = trio[i]
        return (a + da) % NA, (c + dc) % NC

    def c_copy(i):
        oa, oc = trio_at(i)
        return rdma(c_hbm.at[oc], cbuf.at[own_s], c_s.at[i], c_r.at[own_s], d, oa * (NY * NC) + y * NC + oc)

    parts = range(4)

    def x_part(ref, part):
        return ref.at[part // 2, pl.ds(part % 2 * 4, 4)]

    def x_copy(half, away):
        oa, oc = (1 - a, c) if away else (a, 1 - c)
        return rdma(
            x_part(x_hbm, half),
            x_part(xbuf.at[own_s], half),
            x_s.at[half, away],
            x_r.at[own_s, half],
            d,
            oa * (NY * NC) + y * NC + oc,
        )

    far_s = (1 - a) * NC + c

    def x_pass(half):
        return rdma(
            x_part(xbuf.at[far_s], half),
            x_part(xbuf.at[far_s], half),
            x_s.at[half, 2],
            x_r.at[far_s, half],
            d,
            a * (NY * NC) + y * NC + 1 - c,
        )

    for i in range(3):
        c_copy(i).start()
        leaving.append(c_copy(i).wait_send)
    for half in parts:
        x_copy(half, 1).start()
        leaving.append(x_copy(half, 1).wait_send)
    for half in parts:
        x_copy(half, 0).start()
        leaving.append(x_copy(half, 0).wait_send)

    for core in range(NC):

        @pl.loop(0, NB * NZ)
        def _(k, core=core):
            arrived(picked.at[k, core], pick_s.at[0, 0], pick_r.at[k, core])

    owners_load.wait()
    chosen = picked[owners[c]]
    pt[y, :, lanes_own] = chosen[0]
    qt[z, y] = chosen[1]
    order = (4, 3, 5, 2, 6, 1, 7)
    waves = range(2)

    def along_y(k):
        return d, a * (NY * NC) + ((y + k) % NY) * NC + c

    def along_z(k):
        return b * NZ + (z + k) % NZ, f

    def lanes_of(k):
        return pl.ds(pl.multiple_of((z + k) % NZ * LANES, LANES), LANES)

    def tile_of(h, k):
        return qt.at[z, (y + k) % NY] if h else pt.at[y, :, lanes_of(k)]

    def tile_copy(h, k):
        to = along_y(k) if h else along_z(k)
        return rdma(tile_of(h, 0), tile_of(h, 0), tile_s.at[h, k], tile_r.at[h, y if h else z], *to)

    def tile_arrived(h, k):
        arrived(tile_of(h, k), tile_s.at[0, 0], tile_r.at[h, ((y if h else z) + k) % NZ])

    def slab_of(h, k):
        return qt.at[(z + k) % NZ] if h else pt.at[(y + k) % NY]

    def slab_copy(h, k):
        to = along_z(k) if h else along_y(k)
        return rdma(slab_of(h, 0), slab_of(h, 0), slab_s.at[h, k], slab_r.at[h, z if h else y], *to)

    def slab_arrived(h, k):
        arrived(slab_of(h, k), slab_s.at[0, 0], slab_r.at[h, ((z if h else y) + k) % NZ])

    for h in waves:
        for k in order:
            tile_copy(h, k).start()
            leaving.append(tile_copy(h, k).wait_send)
    tokens = NA * NC * cbuf.shape[1]
    loads[1].wait()
    for i in range(3):
        oa, oc = trio_at(i)
        arrived(cbuf.at[oa * NC + oc], c_s.at[0], c_r.at[oa * NC + oc])
    cbuf_t[...] = cbuf[...].reshape(tokens, NZ * LANES).T
    for h in waves:
        for k in order:
            tile_arrived(h, k)
        for k in order:
            slab_copy(h, k).start()
            leaving.append(slab_copy(h, k).wait_send)

    def ring_slot(way, step):
        return (y - step + NY) % NY if way == 0 else (y + step) % NY

    def ring_copy(h, way, step):
        piece = ht.at[ring_slot(way, step - 1), h]
        to = along_y(1 if way == 0 else NY - 1)
        return rdma(piece, piece, h_s.at[h, way, step - 1], h_r.at[h, way, step - 1], *to)

    def ring_arrived(h, way, step):
        arrived(ht.at[ring_slot(way, step), h], h_s.at[0, 0, 0], h_r.at[h, way, step - 1])

    def forward(h, step):
        for way in range(2):
            if step > 1:
                ring_arrived(h, way, step - 1)
            if step < 4 or way == h:
                ring_copy(h, way, step).start()
                leaving.append(ring_copy(h, way, step).wait_send)

    def project(h):
        if h == 0:
            left = pt[...].reshape(NY * 16, NZ * LANES)
        else:
            left = jnp.concatenate([qt[k].reshape(NY * 16, LANES) for k in range(NZ)], axis=1)
        heads = jnp.dot(left, cbuf_t[...], preferred_element_type=jnp.float32)
        ht[y, h] = heads.astype(jnp.bfloat16)

    def product(h, slots, blocks, start):
        left = jnp.concatenate([ht[slot, h] for slot in slots], axis=1)
        for s in blocks:
            right = jnp.concatenate([xbuf[s, :, slot].reshape(tokens, 256) for slot in slots], axis=0)
            part = jnp.dot(left, right, preferred_element_type=jnp.float32)
            acc[h, s] = part if start else acc[h, s] + part

    def rows_of(h):
        block = d // 2
        return qt.at[block] if h else pt.at[:, :, pl.ds(pl.multiple_of(block * LANES, LANES), LANES)]

    def rows_copy(h, i):
        oa, oc = trio_at(i)
        return rdma(
            rows_of(h),
            rows.at[c, a, h],
            rows_s.at[h, i],
            rows_r.at[h, own_s],
            d,
            oa * (NY * NC) + y * NC + oc,
        )

    def pass_on(half):
        arrived(x_part(xbuf.at[far_s], half), x_s.at[0, 0], x_r.at[far_s, half])
        x_pass(half).start()
        leaving.append(x_pass(half).wait_send)

    for h in waves:
        for k in order:
            slab_arrived(h, k)
        project(h)
        forward(h, 1)
    for h in waves:
        for i in range(3):
            rows_copy(h, i).start()
            leaving.append(rows_copy(h, i).wait_send)
        rows[c, a, h] = rows_of(h)[...]
    pass_on(0)
    pass_on(1)
    forward(0, 2)
    forward(1, 2)
    forward(0, 3)
    forward(1, 3)
    pass_on(2)
    pass_on(3)
    sib_s = a * NC + 1 - c
    other_s = (1 - a) * NC + 1 - c
    here, far = (own_s, sib_s), (far_s, other_s)
    near = (y, ring_slot(0, 1), ring_slot(1, 1))
    wide = (ring_slot(0, 2), ring_slot(1, 2), ring_slot(0, 3), ring_slot(1, 3))
    last = (ring_slot(0, 4),)
    loads[0].wait()
    for half in parts:
        arrived(x_part(xbuf.at[sib_s], half), x_s.at[0, 0], x_r.at[sib_s, half])
    product(0, near, here, True)
    forward(0, 4)
    product(1, near, here, True)
    forward(1, 4)
    for half in parts:
        arrived(x_part(xbuf.at[other_s], half), x_s.at[0, 0], x_r.at[other_s, half])

    def b_copy(h, k):
        to = (z + k) % NZ
        return rdma(
            bsend.at[h, to], brecv.at[h, to], b_s.at[h, k], b_r.at[h, to], (1 - b) * NZ + z, f
        )

    def r_copy(h, k, core):
        to = (z + k) % NZ
        return rdma(
            rsend.at[h, to, core],
            rrecv.at[h, c, z],
            r_s.at[h, k, core],
            r_r.at[h, c, z],
            a * NZ + to,
            b * (NY * NC) + y * NC + core,
        )

    def r_self(core):
        return jnp.logical_and(core == c, a == b)

    for h in waves:
        product(h, near, far, True)
        product(h, wide, here + far, False)
    for h in waves:
        ring_arrived(h, h, 4)
        product(h, last, here + far, False)
        for core in range(NC):
            bsend[h, :, core] = acc[h, (1 - b) * NC + core].astype(jnp.bfloat16).reshape(NZ, 16, 256)
        for k in order + (0,):
            b_copy(h, k).start()
            leaving.append(b_copy(h, k).wait_send)

    def both(h, to):
        arrived(brecv.at[h, to], b_s.at[0, 0], b_r.at[h, to])
        mine = [acc[h, b * NC + core, pl.ds(pl.multiple_of(to * 16, 16), 16), :] for core in range(NC)]
        return jnp.stack(mine) + brecv[h, to].astype(jnp.float32)

    for h in waves:
        for k in order + (0,):
            rsend[h, (z + k) % NZ] = both(h, (z + k) % NZ).astype(jnp.bfloat16)
            for core in range(NC):
                if k:
                    r_copy(h, k, core).start()
                    leaving.append(r_copy(h, k, core).wait_send)
                else:

                    @pl.when(jnp.logical_not(r_self(core)))
                    def _(h=h, core=core):
                        r_copy(h, 0, core).start()

                    @pl.when(r_self(core))
                    def _(h=h, core=core):
                        pltpu.make_async_copy(rsend.at[h, z, core], rrecv.at[h, c, z], r_r.at[h, c, z]).start()

    def r_left():
        for h in waves:
            for core in range(NC):

                @pl.when(jnp.logical_not(r_self(core)))
                def _(h=h, core=core):
                    r_copy(h, 0, core).wait_send()

    leaving.append(r_left)
    for i in range(3):
        oa, oc = trio_at(i)
        for h in waves:
            arrived(rows.at[oc, oa, h], rows_s.at[0, 0], rows_r.at[h, oa * NC + oc])
    for m in range(MATS):
        for h in waves:
            rows_t[m, h] = rows[m, :, h].reshape(256, LANES).T
    loads[2].wait()
    loads[3].wait()

    def d_copy(h, k):
        to = along_z(k) if k else ((1 - b) * NZ + z, f)
        return rdma(dirs.at[d, h], dirs.at[d, h], d_s.at[h, k], d_r.at[h, d], *to)

    def d_pass(h, k):
        piece = dirs.at[b * NZ + (z + k) % NZ, h]
        return rdma(
            piece, piece, p_s.at[h, k], d_r.at[h, b * NZ + (z + k) % NZ], (1 - b) * NZ + z, f
        )

    inverse_root = 1.0 / math.sqrt(TOKENS)
    for h in waves:
        for k in (0,) + order:
            for m in range(MATS):
                arrived(rrecv.at[h, m, (z + k) % NZ], r_s.at[0, 0, 0], r_r.at[h, m, (z + k) % NZ])
        block = slice(16 * h, 16 * h + 16)
        projected = jnp.sum(rrecv[h].astype(jnp.float32), axis=1) * inverse_root
        first = beta_first * first_in[:, block] + (1.0 - beta_first) * projected
        second = beta_second * second_in[:, block] + (1.0 - beta_second) * projected * projected
        direction = (
            first / (1.0 - beta_first**STEP) / (jnp.sqrt(second / (1.0 - beta_second**STEP)) + epsilon)
        )
        dirs[d, h] = direction.astype(jnp.bfloat16)
        for k in (0,) + order:
            d_copy(h, k).start()
            leaving.append(d_copy(h, k).wait_send)
        projected_out[:, block] = projected

    for wait in leaving[: len(leaving) - 2 * NZ]:
        wait()
    del leaving[: len(leaving) - 2 * NZ]
    for h in waves:
        for k in order:
            source = b * NZ + (z + k) % NZ
            arrived(dirs.at[source, h], d_s.at[0, 0], d_r.at[h, source])
            d_pass(h, k).start()
            leaving.append(d_pass(h, k).wait_send)
    updates = []
    own_rows = pl.ds(pl.multiple_of((d % 2) * 64, 64), 64)
    for h in waves:
        for k in (0,) + order:
            source = (1 - b) * NZ + (z + k) % NZ
            arrived(dirs.at[source, h], d_s.at[0, 0], d_r.at[h, source])
        updates.append(
            [
                jnp.dot(
                    rows_t[m, h, own_rows, :],
                    dirs[:, h, m].reshape(256, 256),
                    preferred_element_type=jnp.float32,
                )
                for m in range(MATS)
            ]
        )
    for m in range(MATS):
        update_out[m] = updates[0][m] + updates[1][m]

    for wait in leaving:
        wait()


def on_device(layer_input, cotangent, candidates, moment_first, moment_second, owners):
    bf16, f32 = jnp.bfloat16, jnp.float32
    x = layer_input.reshape(NA, NY, 128, 256)
    cand = jnp.swapaxes(candidates[:, 0], 1, 2)
    vmem = pl.BlockSpec(memory_space=pltpu.VMEM)
    hbm = pl.BlockSpec(memory_space=pl.ANY)
    sem = pltpu.SemaphoreType.DMA
    update, projected = pl.pallas_call(
        kernel,
        out_shape=(
            jax.ShapeDtypeStruct((MATS, 64, 256), f32),
            jax.ShapeDtypeStruct((MATS, 32, 256), f32),
        ),
        in_specs=[hbm] * 6,
        out_specs=(vmem, vmem),
        scratch_shapes=[
            pltpu.VMEM((4, NA, NY, 128, 256), bf16),
            pltpu.VMEM((4, 64, 1024), bf16),
            pltpu.VMEM((1024, 256), bf16),
            pltpu.VMEM((16, NC, 16, LANES), bf16),
            pltpu.VMEM((NY, 16, 1024), bf16),
            pltpu.VMEM((NZ, NY, 16, LANES), bf16),
            pltpu.VMEM((NY, 2, 128, 256), bf16),
            pltpu.VMEM((2, 4, 128, 256), f32),
            pltpu.VMEM((2, NZ, NC, 16, 256), bf16),
            pltpu.VMEM((2, NZ, NC, 16, 256), bf16),
            pltpu.VMEM((2, NZ, NC, 16, 256), bf16),
            pltpu.VMEM((2, MATS, NZ, 16, 256), bf16),
            pltpu.VMEM((16, 2, MATS, 16, 256), bf16),
            pltpu.VMEM((MATS, NA, 2, NY, 16, LANES), bf16),
            pltpu.VMEM((MATS, 2, LANES, 256), bf16),
            pltpu.VMEM((MATS, 32, 256), f32),
            pltpu.VMEM((MATS, 32, 256), f32),
            pltpu.SMEM((MATS,), jnp.int32),
            sem((5,)),
            sem((4, 3)),
            sem((4, 4)),
            sem((3,)),
            sem((4,)),
            sem((MATS, 16)),
            sem((16, NC)),
            sem((2, NZ)),
            sem((2, NZ)),
            sem((2, NY)),
            sem((2, NY)),
            sem((2, 3)),
            sem((2, 4)),
            sem((2, 2, 4)),
            sem((2, 2, 4)),
            sem((2, NZ)),
            sem((2, NZ)),
            sem((2, NZ, NC)),
            sem((2, MATS, NZ)),
            sem((2, NZ)),
            sem((2, 16)),
            sem((2, NZ)),
        ],
        compiler_params=pltpu.CompilerParams(
            collective_id=0, has_side_effects=True, vmem_limit_bytes=67043328
        ),
    )(owners, x, cotangent, cand, moment_first, moment_second)
    first = beta_first * moment_first + (1.0 - beta_first) * projected
    second = beta_second * moment_second + (1.0 - beta_second) * projected * projected
    return update.astype(bf16), first, second


def solution(mesh):
    placed = (
        P("dp", "fsdp"),
        P(None, ("dp", "fsdp"), None),
        P(None, "dp", None, "fsdp"),
        P(None, "dp", "fsdp"),
        P(None, "dp", "fsdp"),
        P(),
    )
    return jax.shard_map(
        on_device,
        mesh=mesh,
        in_specs=placed,
        out_specs=(P(None, "dp", "fsdp"), P(None, "dp", "fsdp"), P(None, "dp", "fsdp")),
        check_vma=False,
    )
```

```python
import math

import jax
import jax.numpy as jnp
from jax import lax
from jax.experimental import pallas as pl
from jax.experimental.pallas import tpu as pltpu
from jax.sharding import PartitionSpec as P

MATS = 2
STEP = 10
TOKENS = 32768
NB = 2
NZ = 8
NA = 2
NY = 8
NC = 2
LANES = 128

beta_first = 0.9
beta_second = 0.999
epsilon = 1e-08

MESH = pl.DeviceIdType.MESH


def kernel(
    owners_hbm,
    x_hbm,
    c_hbm,
    cand,
    first_hbm,
    second_hbm,
    update_out,
    projected_out,
    xbuf,
    cbuf,
    cbuf_t,
    picked,
    pt,
    qt,
    ht,
    acc,
    bsend,
    brecv,
    rsend,
    rrecv,
    dirs,
    rows,
    rows_t,
    first_in,
    second_in,
    owners,
    local_sem,
    x_s,
    x_r,
    c_s,
    c_r,
    pick_s,
    pick_r,
    tile_s,
    tile_r,
    slab_s,
    slab_r,
    rows_s,
    rows_r,
    h_s,
    h_r,
    b_s,
    b_r,
    r_s,
    r_r,
    d_s,
    d_r,
    p_s,
):
    d = lax.axis_index("dp")
    f = lax.axis_index("fsdp")
    b, z = d // NZ, d % NZ
    a, y, c = f // (NY * NC), (f // NC) % NY, f % NC
    own_s = a * NC + c

    def rdma(src, dst, send, recv, dp, fsdp):
        return pltpu.make_async_remote_copy(
            src_ref=src, dst_ref=dst, send_sem=send, recv_sem=recv, device_id=(dp, fsdp), device_id_type=MESH
        )

    def arrived(dst, send, recv):
        rdma(dst, dst, send, recv, d, f).wait_recv()

    def sent(src, send, recv):
        rdma(src, src, send, recv, d, f).wait_send()

    barrier = pltpu.get_barrier_semaphore()
    leaving = []

    def greet(dp, fsdp):
        pl.semaphore_signal(barrier, inc=1, device_id=(dp, fsdp), device_id_type=MESH)

    @pl.loop(0, NB * NZ)
    def _(k):
        for core in range(NC):

            @pl.when(jnp.logical_or(k != d, core != c))
            def _():
                greet(k, a * (NY * NC) + y * NC + core)

    for k in range(NB):
        for core in range(NC):
            greet(k * NZ + z, (1 - a) * (NY * NC) + y * NC + core)
    for k in range(1, NY):
        greet(d, a * (NY * NC) + ((y + k) % NY) * NC + c)

    owners_load = pltpu.make_async_copy(owners_hbm, owners, local_sem.at[4])
    owners_load.start()
    loads = [
        pltpu.make_async_copy(x_hbm, xbuf.at[own_s], local_sem.at[0]),
        pltpu.make_async_copy(c_hbm.at[c], cbuf.at[own_s], local_sem.at[1]),
        pltpu.make_async_copy(first_hbm, first_in, local_sem.at[2]),
        pltpu.make_async_copy(second_hbm, second_in, local_sem.at[3]),
    ]
    for load in loads:
        load.start()
    pl.semaphore_wait(barrier, NB * NZ * NC - 1 + NB * NC + NY - 1)

    def pick_copy(m, k):
        return rdma(
            cand.at[m, :, pl.ds(pl.multiple_of((k % NZ) * LANES, LANES), LANES)],
            picked.at[d, c],
            pick_s.at[m, k],
            pick_r.at[d, c],
            k,
            a * (NY * NC) + y * NC + m,
        )

    def pick_self(m, k):
        return jnp.logical_and(c == m, k == d)

    @pl.loop(0, NB * NZ)
    def _(k):
        to = (d + NZ // 2 + k) % (NB * NZ)
        for m in range(MATS):

            @pl.when(jnp.logical_not(pick_self(m, to)))
            def _(m=m):
                pick_copy(m, to).start()

    lanes_own = pl.ds(pl.multiple_of(z * LANES, LANES), LANES)
    pick_own = pltpu.make_async_copy(cand.at[c, :, lanes_own], picked.at[d, c], pick_r.at[d, c])
    pick_own.start()

    def picks_left():
        for m in range(MATS):

            @pl.loop(0, NB * NZ)
            def _(k, m=m):
                @pl.when(jnp.logical_not(pick_self(m, k)))
                def _():
                    pick_copy(m, k).wait_send()

    leaving.append(picks_left)

    trio = ((0, 1), (1, 0), (1, 1))

    def trio_at(i):
        da, dc = trio[i]
        return (a + da) % NA, (c + dc) % NC

    def c_copy(i):
        oa, oc = trio_at(i)
        return rdma(c_hbm.at[oc], cbuf.at[own_s], c_s.at[i], c_r.at[own_s], d, oa * (NY * NC) + y * NC + oc)

    parts = range(4)

    def x_part(ref, part):
        return ref.at[part // 2, pl.ds(part % 2 * 4, 4)]

    def x_copy(half, away):
        oa, oc = (1 - a, c) if away else (a, 1 - c)
        return rdma(
            x_part(x_hbm, half),
            x_part(xbuf.at[own_s], half),
            x_s.at[half, away],
            x_r.at[own_s, half],
            d,
            oa * (NY * NC) + y * NC + oc,
        )

    far_s = (1 - a) * NC + c

    def x_pass(half):
        return rdma(
            x_part(xbuf.at[far_s], half),
            x_part(xbuf.at[far_s], half),
            x_s.at[half, 2],
            x_r.at[far_s, half],
            d,
            a * (NY * NC) + y * NC + 1 - c,
        )

    for i in range(3):
        c_copy(i).start()
        leaving.append(c_copy(i).wait_send)
    for half in parts:
        x_copy(half, 1).start()
        leaving.append(x_copy(half, 1).wait_send)
    for half in parts:
        x_copy(half, 0).start()
        leaving.append(x_copy(half, 0).wait_send)

    for core in range(NC):

        @pl.loop(0, NB * NZ)
        def _(k, core=core):
            arrived(picked.at[k, core], pick_s.at[0, 0], pick_r.at[k, core])

    owners_load.wait()
    chosen = picked[owners[c]]
    pt[y, :, lanes_own] = chosen[0]
    qt[z, y] = chosen[1]
    order = (4, 3, 5, 2, 6, 1, 7)
    waves = range(2)

    def along_y(k):
        return d, a * (NY * NC) + ((y + k) % NY) * NC + c

    def along_z(k):
        return b * NZ + (z + k) % NZ, f

    def lanes_of(k):
        return pl.ds(pl.multiple_of((z + k) % NZ * LANES, LANES), LANES)

    def tile_of(h, k):
        return qt.at[z, (y + k) % NY] if h else pt.at[y, :, lanes_of(k)]

    def tile_copy(h, k):
        to = along_y(k) if h else along_z(k)
        return rdma(tile_of(h, 0), tile_of(h, 0), tile_s.at[h, k], tile_r.at[h, y if h else z], *to)

    def tile_arrived(h, k):
        arrived(tile_of(h, k), tile_s.at[0, 0], tile_r.at[h, ((y if h else z) + k) % NZ])

    def slab_of(h, k):
        return qt.at[(z + k) % NZ] if h else pt.at[(y + k) % NY]

    def slab_copy(h, k):
        to = along_z(k) if h else along_y(k)
        return rdma(slab_of(h, 0), slab_of(h, 0), slab_s.at[h, k], slab_r.at[h, z if h else y], *to)

    def slab_arrived(h, k):
        arrived(slab_of(h, k), slab_s.at[0, 0], slab_r.at[h, ((z if h else y) + k) % NZ])

    for h in waves:
        for k in order:
            tile_copy(h, k).start()
            leaving.append(tile_copy(h, k).wait_send)
    tokens = NA * NC * cbuf.shape[1]
    loads[1].wait()
    for i in range(3):
        oa, oc = trio_at(i)
        arrived(cbuf.at[oa * NC + oc], c_s.at[0], c_r.at[oa * NC + oc])
    cbuf_t[...] = cbuf[...].reshape(tokens, NZ * LANES).T
    for h in waves:
        for k in order:
            tile_arrived(h, k)
        for k in order:
            slab_copy(h, k).start()
            leaving.append(slab_copy(h, k).wait_send)

    def ring_slot(way, step):
        return (y - step + NY) % NY if way == 0 else (y + step) % NY

    def ring_copy(h, way, step):
        piece = ht.at[ring_slot(way, step - 1), h]
        to = along_y(1 if way == 0 else NY - 1)
        return rdma(piece, piece, h_s.at[h, way, step - 1], h_r.at[h, way, step - 1], *to)

    def ring_arrived(h, way, step):
        arrived(ht.at[ring_slot(way, step), h], h_s.at[0, 0, 0], h_r.at[h, way, step - 1])

    def forward(h, step):
        for way in range(2):
            if step > 1:
                ring_arrived(h, way, step - 1)
            if step < 4 or way == h:
                ring_copy(h, way, step).start()
                leaving.append(ring_copy(h, way, step).wait_send)

    def project(h):
        if h == 0:
            left = pt[...].reshape(NY * 16, NZ * LANES)
        else:
            left = jnp.concatenate([qt[k].reshape(NY * 16, LANES) for k in range(NZ)], axis=1)
        heads = jnp.dot(left, cbuf_t[...], preferred_element_type=jnp.float32)
        ht[y, h] = heads.astype(jnp.bfloat16)

    def product(h, slots, blocks, start):
        left = jnp.concatenate([ht[slot, h] for slot in slots], axis=1)
        for s in blocks:
            right = jnp.concatenate([xbuf[s, :, slot].reshape(tokens, 256) for slot in slots], axis=0)
            part = jnp.dot(left, right, preferred_element_type=jnp.float32)
            acc[h, s] = part if start else acc[h, s] + part

    def rows_of(h):
        block = d // 2
        return qt.at[block] if h else pt.at[:, :, pl.ds(pl.multiple_of(block * LANES, LANES), LANES)]

    def rows_copy(h, i):
        oa, oc = trio_at(i)
        return rdma(
            rows_of(h),
            rows.at[c, a, h],
            rows_s.at[h, i],
            rows_r.at[h, own_s],
            d,
            oa * (NY * NC) + y * NC + oc,
        )

    def pass_on(half):
        arrived(x_part(xbuf.at[far_s], half), x_s.at[0, 0], x_r.at[far_s, half])
        x_pass(half).start()
        leaving.append(x_pass(half).wait_send)

    for h in waves:
        for k in order:
            slab_arrived(h, k)
        project(h)
        forward(h, 1)
    for h in waves:
        for i in range(3):
            rows_copy(h, i).start()
            leaving.append(rows_copy(h, i).wait_send)
        rows[c, a, h] = rows_of(h)[...]
    pass_on(0)
    pass_on(1)
    forward(0, 2)
    forward(1, 2)
    forward(0, 3)
    forward(1, 3)
    pass_on(2)
    pass_on(3)
    sib_s = a * NC + 1 - c
    other_s = (1 - a) * NC + 1 - c
    here, far = (own_s, sib_s), (far_s, other_s)
    near = (y, ring_slot(0, 1), ring_slot(1, 1))
    wide = (ring_slot(0, 2), ring_slot(1, 2), ring_slot(0, 3), ring_slot(1, 3))
    last = (ring_slot(0, 4),)
    loads[0].wait()
    for half in parts:
        arrived(x_part(xbuf.at[sib_s], half), x_s.at[0, 0], x_r.at[sib_s, half])
    product(0, near, here, True)
    forward(0, 4)
    product(1, near, here, True)
    forward(1, 4)
    for half in parts:
        arrived(x_part(xbuf.at[other_s], half), x_s.at[0, 0], x_r.at[other_s, half])

    def b_copy(h, k):
        to = (z + k) % NZ
        return rdma(
            bsend.at[h, to], brecv.at[h, to], b_s.at[h, k], b_r.at[h, to], (1 - b) * NZ + z, f
        )

    def r_copy(h, k, core):
        to = (z + k) % NZ
        return rdma(
            rsend.at[h, to, core],
            rrecv.at[h, c, z],
            r_s.at[h, k, core],
            r_r.at[h, c, z],
            a * NZ + to,
            b * (NY * NC) + y * NC + core,
        )

    def r_self(core):
        return jnp.logical_and(core == c, a == b)

    for h in waves:
        product(h, near, far, True)
        product(h, wide, here + far, False)
    for h in waves:
        ring_arrived(h, h, 4)
        product(h, last, here + far, False)
        for core in range(NC):
            bsend[h, :, core] = acc[h, (1 - b) * NC + core].astype(jnp.bfloat16).reshape(NZ, 16, 256)
        for k in order + (0,):
            b_copy(h, k).start()
            leaving.append(b_copy(h, k).wait_send)

    def both(h, to):
        arrived(brecv.at[h, to], b_s.at[0, 0], b_r.at[h, to])
        mine = [acc[h, b * NC + core, pl.ds(pl.multiple_of(to * 16, 16), 16), :] for core in range(NC)]
        return jnp.stack(mine) + brecv[h, to].astype(jnp.float32)

    for h in waves:
        for k in order + (0,):
            rsend[h, (z + k) % NZ] = both(h, (z + k) % NZ).astype(jnp.bfloat16)
            for core in range(NC):
                if k:
                    r_copy(h, k, core).start()
                    leaving.append(r_copy(h, k, core).wait_send)
                else:

                    @pl.when(jnp.logical_not(r_self(core)))
                    def _(h=h, core=core):
                        r_copy(h, 0, core).start()

                    @pl.when(r_self(core))
                    def _(h=h, core=core):
                        pltpu.make_async_copy(rsend.at[h, z, core], rrecv.at[h, c, z], r_r.at[h, c, z]).start()

    def r_left():
        for h in waves:
            for core in range(NC):

                @pl.when(jnp.logical_not(r_self(core)))
                def _(h=h, core=core):
                    r_copy(h, 0, core).wait_send()

    leaving.append(r_left)
    for i in range(3):
        oa, oc = trio_at(i)
        for h in waves:
            arrived(rows.at[oc, oa, h], rows_s.at[0, 0], rows_r.at[h, oa * NC + oc])
    for m in range(MATS):
        for h in waves:
            rows_t[m, h] = rows[m, :, h].reshape(256, LANES).T
    loads[2].wait()
    loads[3].wait()

    def d_copy(h, k):
        to = along_z(k) if k else ((1 - b) * NZ + z, f)
        return rdma(dirs.at[d, h], dirs.at[d, h], d_s.at[h, k], d_r.at[h, d], *to)

    def d_pass(h, k):
        piece = dirs.at[b * NZ + (z + k) % NZ, h]
        return rdma(
            piece, piece, p_s.at[h, k], d_r.at[h, b * NZ + (z + k) % NZ], (1 - b) * NZ + z, f
        )

    inverse_root = 1.0 / math.sqrt(TOKENS)
    for h in waves:
        for k in (0,) + order:
            for m in range(MATS):
                arrived(rrecv.at[h, m, (z + k) % NZ], r_s.at[0, 0, 0], r_r.at[h, m, (z + k) % NZ])
        block = slice(16 * h, 16 * h + 16)
        projected = jnp.sum(rrecv[h].astype(jnp.float32), axis=1) * inverse_root
        first = beta_first * first_in[:, block] + (1.0 - beta_first) * projected
        second = beta_second * second_in[:, block] + (1.0 - beta_second) * projected * projected
        direction = (
            first / (1.0 - beta_first**STEP) / (jnp.sqrt(second / (1.0 - beta_second**STEP)) + epsilon)
        )
        dirs[d, h] = direction.astype(jnp.bfloat16)
        for k in (0,) + order:
            d_copy(h, k).start()
            leaving.append(d_copy(h, k).wait_send)
        projected_out[:, block] = projected

    for wait in leaving[: len(leaving) - 2 * NZ]:
        wait()
    del leaving[: len(leaving) - 2 * NZ]
    for h in waves:
        for k in order:
            source = b * NZ + (z + k) % NZ
            arrived(dirs.at[source, h], d_s.at[0, 0], d_r.at[h, source])
            d_pass(h, k).start()
            leaving.append(d_pass(h, k).wait_send)
    updates = []
    own_rows = pl.ds(pl.multiple_of((d % 2) * 64, 64), 64)
    for h in waves:
        for k in (0,) + order:
            source = (1 - b) * NZ + (z + k) % NZ
            arrived(dirs.at[source, h], d_s.at[0, 0], d_r.at[h, source])
        updates.append(
            [
                jnp.dot(
                    rows_t[m, h, own_rows, :],
                    dirs[:, h, m].reshape(256, 256),
                    preferred_element_type=jnp.float32,
                )
                for m in range(MATS)
            ]
        )
    for m in range(MATS):
        update_out[m] = updates[0][m] + updates[1][m]

    for wait in leaving:
        wait()


def on_device(layer_input, cotangent, candidates, moment_first, moment_second, owners):
    bf16, f32 = jnp.bfloat16, jnp.float32
    x = layer_input.reshape(NA, NY, 128, 256)
    cand = jnp.swapaxes(candidates[:, 0], 1, 2)
    vmem = pl.BlockSpec(memory_space=pltpu.VMEM)
    hbm = pl.BlockSpec(memory_space=pl.ANY)
    sem = pltpu.SemaphoreType.DMA
    update, projected = pl.pallas_call(
        kernel,
        out_shape=(
            jax.ShapeDtypeStruct((MATS, 64, 256), f32),
            jax.ShapeDtypeStruct((MATS, 32, 256), f32),
        ),
        in_specs=[hbm] * 6,
        out_specs=(vmem, vmem),
        scratch_shapes=[
            pltpu.VMEM((4, NA, NY, 128, 256), bf16),
            pltpu.VMEM((4, 64, 1024), bf16),
            pltpu.VMEM((1024, 256), bf16),
            pltpu.VMEM((16, NC, 16, LANES), bf16),
            pltpu.VMEM((NY, 16, 1024), bf16),
            pltpu.VMEM((NZ, NY, 16, LANES), bf16),
            pltpu.VMEM((NY, 2, 128, 256), bf16),
            pltpu.VMEM((2, 4, 128, 256), f32),
            pltpu.VMEM((2, NZ, NC, 16, 256), bf16),
            pltpu.VMEM((2, NZ, NC, 16, 256), bf16),
            pltpu.VMEM((2, NZ, NC, 16, 256), bf16),
            pltpu.VMEM((2, MATS, NZ, 16, 256), bf16),
            pltpu.VMEM((16, 2, MATS, 16, 256), bf16),
            pltpu.VMEM((MATS, NA, 2, NY, 16, LANES), bf16),
            pltpu.VMEM((MATS, 2, LANES, 256), bf16),
            pltpu.VMEM((MATS, 32, 256), f32),
            pltpu.VMEM((MATS, 32, 256), f32),
            pltpu.SMEM((MATS,), jnp.int32),
            sem((5,)),
            sem((4, 3)),
            sem((4, 4)),
            sem((3,)),
            sem((4,)),
            sem((MATS, 16)),
            sem((16, NC)),
            sem((2, NZ)),
            sem((2, NZ)),
            sem((2, NY)),
            sem((2, NY)),
            sem((2, 3)),
            sem((2, 4)),
            sem((2, 2, 4)),
            sem((2, 2, 4)),
            sem((2, NZ)),
            sem((2, NZ)),
            sem((2, NZ, NC)),
            sem((2, MATS, NZ)),
            sem((2, NZ)),
            sem((2, 16)),
            sem((2, NZ)),
        ],
        compiler_params=pltpu.CompilerParams(
            collective_id=0, has_side_effects=True, vmem_limit_bytes=67043328
        ),
    )(owners, x, cotangent, cand, moment_first, moment_second)
    first = beta_first * moment_first + (1.0 - beta_first) * projected
    second = beta_second * moment_second + (1.0 - beta_second) * projected * projected
    return update.astype(bf16), first, second


def solution(mesh):
    placed = (
        P("dp", "fsdp"),
        P(None, ("dp", "fsdp"), None),
        P(None, "dp", None, "fsdp"),
        P(None, "dp", "fsdp"),
        P(None, "dp", "fsdp"),
        P(),
    )
    return jax.shard_map(
        on_device,
        mesh=mesh,
        in_specs=placed,
        out_specs=(P(None, "dp", "fsdp"), P(None, "dp", "fsdp"), P(None, "dp", "fsdp")),
        check_vma=False,
    )
```
